32 devices in a mesh: band: 2 (over x), feed: 16 (over z, y, core).
Axes of the slice: x: 2, y: 2, z: 4, core: 2. Of those that a mesh axis runs over, the one named last changes fastest.
Arguments:
- samples: int32 [8192, 16, 519], P(('band', 'feed')), parts along dimension 0, may hold values from 0 to 255
- gains: int32 [2, 32, 4096], P(None, 'band', 'feed'), parts along dimension 1, may hold values from -2048 to 2047
- feed_slot: int32 [4096], replicated, may hold values from 0 to 4095, each once
Outputs:
- visibility: float32 [8192, 2, 4096], P(('band', 'feed')), parts along dimension 0
The draws below stay inside these ranges and needn't reach their ends.
There are 2 independent parts, one for each index of `band`. The reference program is written for one: setup_inputs(seed, part) draws one part's arguments, and reference() takes and returns one part's arrays. A program takes and returns all parts, laid end to end along the dimension named above; an argument that names none is the same for every part. Nothing has to cross between parts.
Inputs may be any that keep to these rules, and one draw needn't show every extreme that they name: `samples`: each word is 16 times the in-phase level plus the quadrature level, both offset by 8. `feed_slot`: every slot appears once.
All inputs are finite; a program needn't handle non-finite values.
Results may differ from the reference program's by a relative error of at most 0.0026.
Values may be sent and summed in bfloat16 or wider, within the bound.
A program may use at most 128 MiB of HBM per device.

```python
import math
import jax
import jax.numpy as jnp
from jax import lax

INPUTS = 4096
CH = 16
TAPS = 8
SPECTRA = 512
ROWS = 256
QUARTS = 1
NFRAME = 519
N_FEED = 16


def place_ends(entries, own_key, smallest, top_value):
    longest = entries.shape.index(max(entries.shape))
    spots = []
    for shift in (0, 1):
        where = [jax.random.randint(jax.random.fold_in(own_key, axis), (), 0, length) for axis, length in enumerate(entries.shape)]
        where[longest] = (where[longest] + shift) % entries.shape[longest]
        spots.append(tuple(where))
    return entries.at[spots[0]].set(smallest).at[spots[1]].set(top_value)


def setup_inputs(seed: int = 0, part: int = 0) -> dict:
    streams_of = jax.random.split(jax.random.key(seed), 4)
    part_splits = jax.random.split(jax.random.fold_in(streams_of[3], part), 4)
    return {
        "samples": place_ends(jax.random.randint(part_splits[0], (INPUTS, CH, NFRAME), 0, 256), jax.random.fold_in(part_splits[0], 1), 0, 255).astype(jnp.int32),
        "gains": place_ends(jax.random.randint(part_splits[1], (2, CH, INPUTS), -2048, 2048), jax.random.fold_in(part_splits[1], 1), -2048, 2047).astype(jnp.int32),
        "feed_slot": jax.random.permutation(streams_of[2], INPUTS).astype(jnp.int32),
    }


def filter_taps():
    length = TAPS * CH
    place = jnp.arange(length).astype(jnp.float32)
    window = 0.5 - 0.5 * jnp.cos(2.0 * math.pi * place / (length - 1))
    return (jnp.sinc((place - 0.5 * (length - 1)) / CH) * window).reshape(TAPS, CH)

def dft_table():
    index = jnp.arange(CH, dtype=jnp.int32)
    phase = index[:, None] * index[None, :] % CH
    angle = phase.astype(jnp.float32) * (2.0 * math.pi / CH)
    cosine = jnp.cos(angle) / math.sqrt(CH)
    sine = jnp.sin(angle) / math.sqrt(CH)
    upper = jnp.stack([cosine, sine], axis=1)
    lower = jnp.stack([-sine, cosine], axis=1)
    return jnp.stack([upper, lower], axis=0)

def channelize(words, scales, blocks):
    inphase = (words // 16 - 8).astype(jnp.float32) * 0.125
    quadrature = (words % 16 - 8).astype(jnp.float32) * 0.125
    voltage = jnp.stack([inphase, quadrature], axis=1)
    taps = filter_taps()
    count = words.shape[2] - TAPS + 1
    filtered = taps[0][None, None, :, None] * voltage[:, :, :, 0:count]
    for tap in range(1, TAPS):
        filtered = filtered + taps[tap][None, None, :, None] * voltage[:, :, :, tap:tap + count]
    split = filtered.reshape(filtered.shape[0], 2, CH, blocks, count // blocks)
    channels = jnp.einsum('pcqk,nqkat->canpt', dft_table(), split, precision=lax.Precision.HIGHEST)
    gain = scales.astype(jnp.float32) * (1.0 / 2048.0)
    gain_real = gain[0][:, None, :, None]
    gain_imag = gain[1][:, None, :, None]
    real = channels[:, :, :, 0]
    imag = channels[:, :, :, 1]
    weighted = jnp.stack([gain_real * real - gain_imag * imag, gain_real * imag + gain_imag * real], axis=3)
    return weighted.astype(jnp.bfloat16)

def reference(samples, gains, feed_slot):
    width = INPUTS // N_FEED

    def one_tile(first):
        words = lax.dynamic_slice_in_dim(samples, first, width, 0)
        scales = lax.dynamic_slice_in_dim(gains, first, width, 2)
        return channelize(words, scales, 1)[:, 0]
    firsts = jnp.arange(N_FEED, dtype=jnp.int32) * width
    tiles = lax.map(one_tile, firsts)
    weighted = jnp.transpose(tiles, (1, 0, 2, 3, 4)).reshape(CH, INPUTS, 2 * SPECTRA)
    span = QUARTS * ROWS

    def one_channel(channel_block):
        ordered = jnp.take(channel_block, feed_slot, axis=0)
        feed_rows = ordered[:span]
        real = feed_rows[:, :SPECTRA]
        imag = feed_rows[:, SPECTRA:]
        left_side = jnp.stack([feed_rows, jnp.concatenate([imag, -real], axis=1)], axis=1)
        left_side = left_side.reshape(2 * span, 2 * SPECTRA)
        product = jnp.dot(left_side, ordered.T, preferred_element_type=jnp.float32)
        return product.reshape(span, 2, INPUTS) * (1.0 / SPECTRA)
    visibility = lax.map(one_channel, weighted)
    return visibility.reshape(N_FEED * ROWS, 2, INPUTS)
```

```python
import functools
import math

import jax
import jax.numpy as jnp
import numpy as np
from jax import lax
from jax.experimental import pallas as pl
from jax.experimental.pallas import tpu as pltpu
from jax.sharding import PartitionSpec as P

CH = 16
TAPS = 8
SPECTRA = 512
ROWS = 256
SHARES = (4, 5, 5, 2)
SPLIT_SHARES = (2, 3, 2, 1)
SPAN = 32
TILE = 512
TERMS = 3
LANES = 128


def filter_bank():
    length = TAPS * CH
    place = np.arange(length, dtype=np.float64)
    window = 0.5 - 0.5 * np.cos(2.0 * math.pi * place / (length - 1))
    taps = (np.sinc((place - 0.5 * (length - 1)) / CH) * window).reshape(TAPS, CH)
    index = np.arange(CH)
    angle = (index[:, None] * index[None, :] % CH) * (2.0 * math.pi / CH)
    cosine = np.cos(angle) / math.sqrt(CH)
    sine = np.sin(angle) / math.sqrt(CH)
    table = np.stack([np.stack([cosine, sine], 1), np.stack([-sine, cosine], 1)], 0)
    bank = table[:, :, None, :, :] * taps[None, None, :, None, :]
    bank = 0.125 * bank.reshape(2 * CH, TAPS * 2 * CH)
    terms = []
    for _ in range(TERMS):
        term = bank.astype(jnp.bfloat16)
        terms.append(term)
        bank = bank - term.astype(np.float64)
    return np.concatenate(terms, 0)


def unpack(words):
    inphase = ((words >> 4) - 8).astype(jnp.float32).astype(jnp.bfloat16)
    quadrature = ((words & 15) - 8).astype(jnp.float32).astype(jnp.bfloat16)
    return jnp.concatenate([inphase, quadrature], axis=0)


def pick(moved_ref, columns, first=0):
    sources, _, width = moved_ref.shape
    total = None
    for source in range(sources):
        place = lax.broadcasted_iota(jnp.int32, (width, columns.shape[1]), 0) + (source * width + first)
        hot = jnp.where(place == columns, 1.0, 0.0).astype(jnp.bfloat16)
        part = jnp.dot(moved_ref[source], hot, preferred_element_type=jnp.float32)
        total = part if total is None else total + part
    return total


def put_left(left, picked, scale):
    depth = picked.shape[0]
    feed_rows = jnp.transpose(picked) * scale
    real, imag = feed_rows[:, : depth // 2], feed_rows[:, depth // 2 :]
    left[0, :, :depth] = jnp.concatenate([real, imag], axis=1).astype(jnp.bfloat16)
    left[1, :, :depth] = jnp.concatenate([imag, -real], axis=1).astype(jnp.bfloat16)


def set_left(left, moved_ref, columns, scale):
    put_left(left, pick(moved_ref, columns), scale)


def channelize(count, bank, gain, words, out, voltage, rows):
    inputs = out.shape[2]

    def block(i, carry):
        base = i * SPAN
        for m in range(SPAN + TAPS - 1):
            voltage[m * 2 * CH : (m + 1) * 2 * CH, :] = unpack(words[base + m])
        for s in range(SPAN):
            window = voltage[s * 2 * CH : (s + TAPS) * 2 * CH, :]
            parts = jnp.dot(bank, window, preferred_element_type=jnp.float32)
            whole = parts[: 2 * CH]
            for term in range(1, TERMS):
                whole = whole + parts[2 * CH * term : 2 * CH * (term + 1)]
            real, imag = whole[:CH], whole[CH:]
            upper = gain[0] * real - gain[1] * imag
            lower = gain[0] * imag + gain[1] * real
            for lane in range(rows.shape[1]):
                place = slice(lane * LANES, (lane + 1) * LANES)
                rows[0, lane, s * CH : (s + 1) * CH, :] = upper[:, place]
                rows[1, lane, s * CH : (s + 1) * CH, :] = lower[:, place]
        for c in range(CH):
            for part in range(2):
                where = pl.ds(pl.multiple_of(part * count + base, SPAN), SPAN)
                for lane in range(rows.shape[1]):
                    width = min(LANES, inputs - lane * LANES)
                    piece = rows[part, lane, pl.ds(c, SPAN, stride=CH), :]
                    out[c, where, lane * LANES : lane * LANES + width] = piece[:, :width].astype(
                        jnp.bfloat16
                    )
        return carry

    lax.fori_loop(0, count // SPAN, block, 0)


def exchange_kernel(counts, groups, scale, bank_ref, words_hbm, gains_ref, slot_ref, own_ref, *refs):
    chunks = len(counts)
    last_hbm, total_hbm = refs[:2]
    words_bufs = refs[2 : 2 + chunks]
    send_bufs = refs[2 + chunks : 2 + 2 * chunks]
    hold_bufs = refs[2 + 2 * chunks : 1 + 3 * chunks]
    voltage, rows, total, left, word_sem, own_sem, total_sem, send_sem, recv_sem = refs[1 + 3 * chunks :]
    targets = hold_bufs + (last_hbm,)
    me = lax.axis_index("feed")
    size = lax.axis_size("feed")
    bank = bank_ref[...]
    gain = gains_ref[...].astype(jnp.float32) * (1.0 / 2048.0)

    barrier = pltpu.get_barrier_semaphore()

    def greet(d, carry):
        pl.semaphore_signal(
            barrier, inc=1, device_id={"feed": (me + d) % size}, device_id_type=pl.DeviceIdType.MESH
        )
        return carry

    lax.fori_loop(1, size, greet, 0)

    def word_copy(k):
        source = words_hbm.at[pl.ds(sum(counts[:k]), counts[k] + TAPS - 1)]
        return pltpu.make_async_copy(source, words_bufs[k], word_sem.at[k])

    def own_copy(k):
        return pltpu.make_async_copy(send_bufs[k].at[me // groups], targets[k].at[me], own_sem.at[k])

    def remote(k, d):
        there = (me + d) % size
        return pltpu.make_async_remote_copy(
            src_ref=send_bufs[k].at[there // groups],
            dst_ref=targets[k].at[me],
            send_sem=send_sem.at[k, d],
            recv_sem=recv_sem.at[k, d],
            device_id={"feed": there},
            device_id_type=pl.DeviceIdType.MESH,
        )

    def send(k):
        def one(d, carry):
            remote(k, d).start()
            return carry

        lax.fori_loop(1, size, one, 0)
        own_copy(k).start()

    def arrive(k):
        def one(d, carry):
            remote(k, d).wait_recv()
            return carry

        own_copy(k).wait()
        lax.fori_loop(1, size, one, 0)

    def drain(k):
        def one(d, carry):
            remote(k, d).wait_send()
            return carry

        lax.fori_loop(1, size, one, 0)

    for k in range(chunks):
        word_copy(k).start()
    for k in range(chunks):
        word_copy(k).wait()
        channelize(counts[k], bank, gain, words_bufs[k], send_bufs[k], voltage, rows)
        if k == 0:
            pl.semaphore_wait(barrier, size - 1)
        send(k)

    feeds = slot_ref.shape[1]
    tile = min(TILE, feeds)
    for k in range(chunks - 1):
        arrive(k)
        depth = 2 * counts[k]
        set_left(left, hold_bufs[k], own_ref[...], scale)

        def columns(j, carry, k=k, depth=depth):
            where = pl.ds(pl.multiple_of(j * tile, tile), tile)
            ordered = pick(hold_bufs[k], slot_ref[:, where]).astype(jnp.bfloat16)
            for part in range(2):
                product = jnp.dot(left[part, :, :depth], ordered, preferred_element_type=jnp.float32)
                if k:
                    product = product + total[part, :, where]
                total[part, :, where] = product
            return carry

        lax.fori_loop(0, feeds // tile, columns, 0)
    total_copy = pltpu.make_async_copy(total, total_hbm, total_sem)
    total_copy.start()
    arrive(chunks - 1)
    for k in range(chunks):
        drain(k)
    total_copy.wait()


def exchange(words, gains, feed_slot, own, counts, inputs, groups, scale):
    size = CH * groups
    feeds = feed_slot.shape[0]
    wide = words.shape[2]
    bank = jnp.asarray(filter_bank())
    held = [jax.ShapeDtypeStruct((size, 2 * count, inputs), jnp.bfloat16) for count in counts]
    memory = pl.BlockSpec(memory_space=pltpu.VMEM)
    anywhere = pl.BlockSpec(memory_space=pl.ANY)
    chunks = len(counts)
    return pl.pallas_call(
        functools.partial(exchange_kernel, counts, groups, scale),
        out_shape=(held[-1], jax.ShapeDtypeStruct((2, ROWS, feeds), jnp.float32)),
        in_specs=[memory, anywhere, memory, memory, memory],
        out_specs=(anywhere, anywhere),
        scratch_shapes=[pltpu.VMEM((count + TAPS - 1, CH, wide), jnp.int32) for count in counts]
        + [pltpu.VMEM((CH, 2 * count, inputs), jnp.bfloat16) for count in counts]
        + [pltpu.VMEM(one.shape, one.dtype) for one in held[:-1]]
        + [
            pltpu.VMEM(((SPAN + TAPS) * 2 * CH, wide), jnp.bfloat16),
            pltpu.VMEM((2, wide // LANES, SPAN * CH, LANES), jnp.float32),
            pltpu.VMEM((2, ROWS, feeds), jnp.float32),
            pltpu.VMEM((2, ROWS, 2 * max(counts)), jnp.bfloat16),
            pltpu.SemaphoreType.DMA((chunks,)),
            pltpu.SemaphoreType.DMA((chunks,)),
            pltpu.SemaphoreType.DMA,
            pltpu.SemaphoreType.DMA((chunks, size)),
            pltpu.SemaphoreType.DMA((chunks, size)),
        ],
        compiler_params=pltpu.CompilerParams(
            collective_id=0, has_side_effects=True, vmem_limit_bytes=60 * 2**20
        ),
    )(bank, words, gains, feed_slot[None], own[None])


def finish_kernel(scale, moved_ref, slot_ref, own_ref, total_ref, out_ref, left):
    @pl.when(pl.program_id(0) == 0)
    def _():
        set_left(left, moved_ref, own_ref[...], scale)

    ordered = pick(moved_ref, slot_ref[...]).astype(jnp.bfloat16)
    for part in range(2):
        product = jnp.dot(left[part], ordered, preferred_element_type=jnp.float32)
        out_ref[:, part, :] = product + total_ref[part]


def split_kernel(counts, scale, bank_ref, words_hbm, gains_ref, slot_ref, own_ref, *refs):
    chunks = len(counts)
    refs = list(refs)

    def take(count):
        taken = refs[:count]
        del refs[:count]
        return taken

    last_hbm, total_hbm = take(2)
    words_bufs = take(chunks)
    send_bufs = take(chunks)
    full_bufs = take(chunks - 1)
    half_bufs = take(chunks)
    give_bufs = take(chunks)
    take_bufs = take(chunks)
    lefts = take(chunks)
    mine, theirs, voltage, rows, total, left = take(6)
    word_sem, own_sem, total_sem, near_sems, cross_sems, row_sems, product_sems = refs
    targets = full_bufs + [last_hbm]
    me = lax.axis_index("feed")
    size = lax.axis_size("feed")
    half = size // 2
    core = me % 2
    base = me // half * half
    away = half - base
    spot = me - base
    mate = away + spot + 1 - 2 * core
    quarter = me // (size // 4)
    inner = (quarter + 1) // 2 % 2
    inputs = send_bufs[0].shape[2]
    bank = bank_ref[...]
    gain = gains_ref[...].astype(jnp.float32) * (1.0 / 2048.0)

    barrier = pltpu.get_barrier_semaphore()

    def greet(d, carry):
        pl.semaphore_signal(
            barrier, inc=1, device_id={"feed": (me + d) % size}, device_id_type=pl.DeviceIdType.MESH
        )
        return carry

    lax.fori_loop(1, size, greet, 0)

    def loop(first, last, step):
        def one(i, carry):
            step(i)
            return carry

        lax.fori_loop(first, last, one, 0)

    def word_copy(k):
        source = words_hbm.at[pl.ds(sum(counts[:k]), counts[k] + TAPS - 1)]
        return pltpu.make_async_copy(source, words_bufs[k], word_sem.at[k])

    def remote(source, target, sems, place, there):
        send_sem, recv_sem = sems
        return pltpu.make_async_remote_copy(
            src_ref=source,
            dst_ref=target,
            send_sem=send_sem.at[place],
            recv_sem=recv_sem.at[place],
            device_id={"feed": there},
            device_id_type=pl.DeviceIdType.MESH,
        )

    def channel(place):
        odd = place % 2
        return (base + place) * (1 - odd) + (away + place - 1) * odd

    def near(k, d):
        place = (spot + d) % half
        return remote(
            send_bufs[k].at[channel(place)], half_bufs[k].at[spot], near_sems, (k, d), base + place
        )

    def near_own(k):
        return pltpu.make_async_copy(send_bufs[k].at[channel(spot)], half_bufs[k].at[spot], own_sem.at[0, k])

    def far(k, i):
        there = away + (spot + i) % half
        return remote(send_bufs[k].at[there], targets[k].at[me], cross_sems, (k, half + i), there)

    def close(k, i):
        there = base + (spot + i) % half
        return remote(send_bufs[k].at[there], targets[k].at[me], cross_sems, (k, i), there)

    def cross_own(k):
        return pltpu.make_async_copy(send_bufs[k].at[me], targets[k].at[me], own_sem.at[1, k])

    def row_copy(k):
        return remote(give_bufs[k], take_bufs[k], row_sems, k, mate)

    def product_copy(j):
        return remote(mine.at[j], theirs.at[j], product_sems, j, mate)

    def send_near(k):
        loop(1, half, lambda d: near(k, d).start())
        near_own(k).start()

    def arrive_near(k):
        near_own(k).wait()
        loop(1, half, lambda d: near(k, d).wait_recv())

    def send_cross(k):
        loop(0, half // 2, lambda q: far(k, 2 * q + 1 - core).start())
        loop(core, half // 2, lambda q: close(k, 2 * q + 1 - core).start())

    def drain(k):
        loop(1, half, lambda d: near(k, d).wait_send())
        loop(0, half // 2, lambda q: far(k, 2 * q + 1 - core).wait_send())
        loop(core, half // 2, lambda q: close(k, 2 * q + 1 - core).wait_send())
        row_copy(k).wait_send()

    def arrive_cross(k):
        cross_own(k).start()
        cross_own(k).wait()
        loop(1, half, lambda i: close(k, i).wait_recv())
        loop(0, half, lambda i: far(k, i).wait_recv())

    for k in range(chunks):
        word_copy(k).start()
    for k in range(chunks):
        word_copy(k).wait()
        channelize(counts[k], bank, gain, words_bufs[k], send_bufs[k], voltage, rows)
        if k == 0:
            pl.semaphore_wait(barrier, size - 1)
        send_near(k)

        @pl.when(inner == 1)
        def _(k=k):
            send_cross(k)

    early = chunks // 2
    for k in range(chunks):
        arrive_near(k)
        give_bufs[k][...] = pick(half_bufs[k], own_ref[...], base * inputs).astype(jnp.bfloat16)
        row_copy(k).start()

    @pl.when(inner == 0)
    def _():
        for k in range(early):
            send_cross(k)

    @pl.when((inner == 0) & (core == 0))
    def _():
        for k in range(early, chunks):
            send_cross(k)

    for k in range(chunks):
        row_copy(k).wait_recv()
        both = give_bufs[k][...].astype(jnp.float32) + take_bufs[k][...].astype(jnp.float32)
        put_left(lefts[k], both, scale)

    def multiply(j):
        for part in range(2):
            product = None
            for k in range(chunks):
                term = jnp.dot(lefts[k][part], half_bufs[k][j], preferred_element_type=jnp.float32)
                product = term if product is None else product + term
            mine[j, part * ROWS : (part + 1) * ROWS, :] = product.astype(jnp.bfloat16)

        @pl.when(core == 1)
        def _():
            product_copy(j).start()

    loop(0, half, multiply)

    @pl.when((inner == 0) & (core == 1))
    def _():
        for k in range(early, chunks):
            send_cross(k)

    feeds = slot_ref.shape[1]
    tile = min(TILE, feeds)

    @pl.when(core == 0)
    def _():
        def place_mine(j):
            where = pl.ds(pl.multiple_of(j * tile, tile), tile)
            ordered = pick(mine, slot_ref[:, where], base * inputs)
            total[0, :, where] = ordered[:ROWS]
            total[1, :, where] = ordered[ROWS:]

        def place_theirs(j):
            where = pl.ds(pl.multiple_of(j * tile, tile), tile)
            ordered = pick(theirs, slot_ref[:, where], away * inputs)
            total[0, :, where] = total[0, :, where] + ordered[:ROWS]
            total[1, :, where] = total[1, :, where] + ordered[ROWS:]

        loop(0, feeds // tile, place_mine)
        loop(0, half, lambda j: product_copy(j).wait_recv())
        loop(0, feeds // tile, place_theirs)

    @pl.when(core == 1)
    def _():
        for k in range(chunks - 1):
            arrive_cross(k)
            depth = 2 * counts[k]
            set_left(left, full_bufs[k], own_ref[...], scale)

            def columns(j, k=k, depth=depth):
                where = pl.ds(pl.multiple_of(j * tile, tile), tile)
                ordered = pick(full_bufs[k], slot_ref[:, where]).astype(jnp.bfloat16)
                for part in range(2):
                    product = jnp.dot(left[part, :, :depth], ordered, preferred_element_type=jnp.float32)
                    if k:
                        product = product + total[part, :, where]
                    total[part, :, where] = product

            loop(0, feeds // tile, columns)

    total_copy = pltpu.make_async_copy(total, total_hbm, total_sem)
    total_copy.start()

    @pl.when(core == 1)
    def _():
        arrive_cross(chunks - 1)
        loop(0, half, lambda j: product_copy(j).wait_send())

    for k in range(chunks):
        drain(k)
    total_copy.wait()


def split_exchange(words, gains, feed_slot, own, counts, inputs, scale):
    size = CH
    half = size // 2
    feeds = feed_slot.shape[0]
    wide = words.shape[2]
    bank = jnp.asarray(filter_bank())
    memory = pl.BlockSpec(memory_space=pltpu.VMEM)
    anywhere = pl.BlockSpec(memory_space=pl.ANY)
    chunks = len(counts)
    half_type = jnp.bfloat16
    return pl.pallas_call(
        functools.partial(split_kernel, counts, scale),
        out_shape=(
            jax.ShapeDtypeStruct((size, 2 * counts[-1], inputs), jnp.bfloat16),
            jax.ShapeDtypeStruct((2, ROWS, feeds), jnp.float32),
        ),
        in_specs=[memory, anywhere, memory, memory, memory],
        out_specs=(anywhere, anywhere),
        scratch_shapes=[pltpu.VMEM((count + TAPS - 1, CH, wide), jnp.int32) for count in counts]
        + [pltpu.VMEM((CH, 2 * count, inputs), half_type) for count in counts]
        + [pltpu.VMEM((size, 2 * count, inputs), half_type) for count in counts[:-1]]
        + [pltpu.VMEM((half, 2 * count, inputs), half_type) for count in counts]
        + [pltpu.VMEM((2 * count, ROWS), half_type) for count in counts] * 2
        + [pltpu.VMEM((2, ROWS, 2 * count), half_type) for count in counts]
        + [
            pltpu.VMEM((half, 2 * ROWS, inputs), half_type),
            pltpu.VMEM((half, 2 * ROWS, inputs), half_type),
            pltpu.VMEM(((SPAN + TAPS) * 2 * CH, wide), half_type),
            pltpu.VMEM((2, wide // LANES, SPAN * CH, LANES), jnp.float32),
            pltpu.VMEM((2, ROWS, feeds), jnp.float32),
            pltpu.VMEM((2, ROWS, 2 * max(counts)), half_type),
            pltpu.SemaphoreType.DMA((chunks,)),
            pltpu.SemaphoreType.DMA((2, chunks)),
            pltpu.SemaphoreType.DMA,
            (pltpu.SemaphoreType.DMA((chunks, half)),) * 2,
            (pltpu.SemaphoreType.DMA((chunks, size)),) * 2,
            (pltpu.SemaphoreType.DMA((chunks,)),) * 2,
            (pltpu.SemaphoreType.DMA((half,)),) * 2,
        ],
        compiler_params=pltpu.CompilerParams(
            collective_id=0, has_side_effects=True, vmem_limit_bytes=60 * 2**20
        ),
    )(bank, words, gains, feed_slot[None], own[None])


def split_finish_kernel(scale, moved_ref, slot_ref, own_ref, total_ref, out_ref, left):
    core = lax.axis_index("feed") % 2

    @pl.when(core == 0)
    def _():
        for part in range(2):
            out_ref[:, part, :] = total_ref[part]

    @pl.when(core == 1)
    def _():
        finish_kernel(scale, moved_ref, slot_ref, own_ref, total_ref, out_ref, left)


def finish(kernel, moved, feed_slot, own, total, scale):
    feeds = feed_slot.shape[0]
    tile = min(TILE, feeds)
    return pl.pallas_call(
        functools.partial(kernel, scale),
        out_shape=jax.ShapeDtypeStruct((ROWS, 2, feeds), jnp.float32),
        grid=(feeds // tile,),
        in_specs=[
            pl.BlockSpec(moved.shape, lambda j: (0, 0, 0)),
            pl.BlockSpec((1, tile), lambda j: (0, j)),
            pl.BlockSpec((1, ROWS), lambda j: (0, 0)),
            pl.BlockSpec((2, ROWS, tile), lambda j: (0, 0, j)),
        ],
        out_specs=pl.BlockSpec((ROWS, 2, tile), lambda j: (0, 0, j)),
        scratch_shapes=[pltpu.VMEM((2, ROWS, moved.shape[1]), jnp.bfloat16)],
    )(moved, feed_slot[None], own[None], total)


def body(samples, gains, feed_slot):
    groups = lax.axis_size("feed") // CH
    first = lax.axis_index("feed") % groups * ROWS
    inputs = samples.shape[0]
    spectra = samples.shape[2] - TAPS + 1
    split = groups == 1 and inputs % LANES == 0
    shares = SPLIT_SHARES if split else SHARES
    counts = tuple(spectra * share // sum(shares) for share in shares)
    words = jnp.transpose(samples, (2, 1, 0))
    spare = -inputs % LANES
    if spare:
        words = jnp.pad(words, ((0, 0), (0, 0), (0, spare)))
        gains = jnp.pad(gains, ((0, 0), (0, 0), (0, spare)))
    own = lax.dynamic_slice_in_dim(feed_slot, first, ROWS, 0)
    scale = 1.0 / spectra
    if split:
        moved, total = split_exchange(words, gains, feed_slot, own, counts, inputs, scale)
        return finish(split_finish_kernel, moved, feed_slot, own, total, scale)
    moved, total = exchange(words, gains, feed_slot, own, counts, inputs, groups, scale)
    return finish(finish_kernel, moved, feed_slot, own, total, scale)


def solution(mesh):
    return jax.shard_map(
        body,
        mesh=mesh,
        in_specs=(P(("band", "feed"), None, None), P(None, "band", "feed"), P()),
        out_specs=P(("band", "feed"), None, None),
        check_vma=False,
    )
```

```python
import functools
import math

import jax
import jax.numpy as jnp
import numpy as np
from jax import lax
from jax.experimental import pallas as pl
from jax.experimental.pallas import tpu as pltpu
from jax.sharding import PartitionSpec as P

CH = 16
TAPS = 8
SPECTRA = 512
ROWS = 256
SHARES = (4, 5, 5, 2)
SPLIT_SHARES = (2, 3, 2, 1)
SPAN = 32
TILE = 512
TERMS = 3
LANES = 128
ROWS_SENT, PRODUCTS_SENT = 100, 101


def issue_plan():
    kinds = ("straight", "across", "close")
    chunks = range(len(SPLIT_SHARES))
    last = chunks[-1]
    plan = {}
    for core in range(2):
        inner = [(k, "straight", k) for k in chunks] + [(last, "across", k) for k in chunks]
        inner += [(PRODUCTS_SENT if core else ROWS_SENT, "close", k) for k in chunks]
        outer = []
        for k in chunks:
            stage = last if k < 2 - core else PRODUCTS_SENT if core else ROWS_SENT
            outer += [(stage, kind, k) for kind in kinds]
        plan[2 + core] = inner
        plan[core] = outer
    return plan


ISSUE = issue_plan()


def filter_bank():
    length = TAPS * CH
    place = np.arange(length, dtype=np.float64)
    window = 0.5 - 0.5 * np.cos(2.0 * math.pi * place / (length - 1))
    taps = (np.sinc((place - 0.5 * (length - 1)) / CH) * window).reshape(TAPS, CH)
    index = np.arange(CH)
    angle = (index[:, None] * index[None, :] % CH) * (2.0 * math.pi / CH)
    cosine = np.cos(angle) / math.sqrt(CH)
    sine = np.sin(angle) / math.sqrt(CH)
    table = np.stack([np.stack([cosine, sine], 1), np.stack([-sine, cosine], 1)], 0)
    bank = table[:, :, None, :, :] * taps[None, None, :, None, :]
    bank = 0.125 * bank.reshape(2 * CH, TAPS * 2 * CH)
    terms = []
    for _ in range(TERMS):
        term = bank.astype(jnp.bfloat16)
        terms.append(term)
        bank = bank - term.astype(np.float64)
    return np.concatenate(terms, 0)


def unpack(words):
    inphase = ((words >> 4) - 8).astype(jnp.float32).astype(jnp.bfloat16)
    quadrature = ((words & 15) - 8).astype(jnp.float32).astype(jnp.bfloat16)
    return jnp.concatenate([inphase, quadrature], axis=0)


def pick(moved_ref, columns, first=0):
    sources, _, width = moved_ref.shape
    total = None
    for source in range(sources):
        place = lax.broadcasted_iota(jnp.int32, (width, columns.shape[1]), 0) + (source * width + first)
        hot = jnp.where(place == columns, 1.0, 0.0).astype(jnp.bfloat16)
        part = jnp.dot(moved_ref[source], hot, preferred_element_type=jnp.float32)
        total = part if total is None else total + part
    return total


def put_left(left, picked, scale):
    depth = picked.shape[0]
    feed_rows = jnp.transpose(picked) * scale
    real, imag = feed_rows[:, : depth // 2], feed_rows[:, depth // 2 :]
    left[0, :, :depth] = jnp.concatenate([real, imag], axis=1).astype(jnp.bfloat16)
    left[1, :, :depth] = jnp.concatenate([imag, -real], axis=1).astype(jnp.bfloat16)


def set_left(left, moved_ref, columns, scale):
    put_left(left, pick(moved_ref, columns), scale)


def channelize(count, bank, gain, words, out, voltage, rows):
    inputs = out.shape[2]

    def block(i, carry):
        base = i * SPAN
        for m in range(SPAN + TAPS - 1):
            voltage[m * 2 * CH : (m + 1) * 2 * CH, :] = unpack(words[base + m])
        for s in range(SPAN):
            window = voltage[s * 2 * CH : (s + TAPS) * 2 * CH, :]
            parts = jnp.dot(bank, window, preferred_element_type=jnp.float32)
            whole = parts[: 2 * CH]
            for term in range(1, TERMS):
                whole = whole + parts[2 * CH * term : 2 * CH * (term + 1)]
            real, imag = whole[:CH], whole[CH:]
            upper = gain[0] * real - gain[1] * imag
            lower = gain[0] * imag + gain[1] * real
            for lane in range(rows.shape[1]):
                place = slice(lane * LANES, (lane + 1) * LANES)
                rows[0, lane, s * CH : (s + 1) * CH, :] = upper[:, place]
                rows[1, lane, s * CH : (s + 1) * CH, :] = lower[:, place]
        for c in range(CH):
            for part in range(2):
                where = pl.ds(pl.multiple_of(part * count + base, SPAN), SPAN)
                for lane in range(rows.shape[1]):
                    width = min(LANES, inputs - lane * LANES)
                    piece = rows[part, lane, pl.ds(c, SPAN, stride=CH), :]
                    out[c, where, lane * LANES : lane * LANES + width] = piece[:, :width].astype(
                        jnp.bfloat16
                    )
        return carry

    lax.fori_loop(0, count // SPAN, block, 0)


def exchange_kernel(counts, groups, scale, bank_ref, words_hbm, gains_ref, slot_ref, own_ref, *refs):
    chunks = len(counts)
    last_hbm, total_hbm = refs[:2]
    words_bufs = refs[2 : 2 + chunks]
    send_bufs = refs[2 + chunks : 2 + 2 * chunks]
    hold_bufs = refs[2 + 2 * chunks : 1 + 3 * chunks]
    voltage, rows, total, left, word_sem, own_sem, total_sem, send_sem, recv_sem = refs[1 + 3 * chunks :]
    targets = hold_bufs + (last_hbm,)
    me = lax.axis_index("feed")
    size = lax.axis_size("feed")
    bank = bank_ref[...]
    gain = gains_ref[...].astype(jnp.float32) * (1.0 / 2048.0)

    barrier = pltpu.get_barrier_semaphore()

    def greet(d, carry):
        pl.semaphore_signal(
            barrier, inc=1, device_id={"feed": (me + d) % size}, device_id_type=pl.DeviceIdType.MESH
        )
        return carry

    lax.fori_loop(1, size, greet, 0)

    def word_copy(k):
        source = words_hbm.at[pl.ds(sum(counts[:k]), counts[k] + TAPS - 1)]
        return pltpu.make_async_copy(source, words_bufs[k], word_sem.at[k])

    def own_copy(k):
        return pltpu.make_async_copy(send_bufs[k].at[me // groups], targets[k].at[me], own_sem.at[k])

    def remote(k, d):
        there = (me + d) % size
        return pltpu.make_async_remote_copy(
            src_ref=send_bufs[k].at[there // groups],
            dst_ref=targets[k].at[me],
            send_sem=send_sem.at[k, d],
            recv_sem=recv_sem.at[k, d],
            device_id={"feed": there},
            device_id_type=pl.DeviceIdType.MESH,
        )

    def send(k):
        def one(d, carry):
            remote(k, d).start()
            return carry

        lax.fori_loop(1, size, one, 0)
        own_copy(k).start()

    def arrive(k):
        def one(d, carry):
            remote(k, d).wait_recv()
            return carry

        own_copy(k).wait()
        lax.fori_loop(1, size, one, 0)

    def drain(k):
        def one(d, carry):
            remote(k, d).wait_send()
            return carry

        lax.fori_loop(1, size, one, 0)

    for k in range(chunks):
        word_copy(k).start()
    for k in range(chunks):
        word_copy(k).wait()
        channelize(counts[k], bank, gain, words_bufs[k], send_bufs[k], voltage, rows)
        if k == 0:
            pl.semaphore_wait(barrier, size - 1)
        send(k)

    feeds = slot_ref.shape[1]
    tile = min(TILE, feeds)
    for k in range(chunks - 1):
        arrive(k)
        depth = 2 * counts[k]
        set_left(left, hold_bufs[k], own_ref[...], scale)

        def columns(j, carry, k=k, depth=depth):
            where = pl.ds(pl.multiple_of(j * tile, tile), tile)
            ordered = pick(hold_bufs[k], slot_ref[:, where]).astype(jnp.bfloat16)
            for part in range(2):
                product = jnp.dot(left[part, :, :depth], ordered, preferred_element_type=jnp.float32)
                if k:
                    product = product + total[part, :, where]
                total[part, :, where] = product
            return carry

        lax.fori_loop(0, feeds // tile, columns, 0)
    total_copy = pltpu.make_async_copy(total, total_hbm, total_sem)
    total_copy.start()
    arrive(chunks - 1)
    for k in range(chunks):
        drain(k)
    total_copy.wait()


def exchange(words, gains, feed_slot, own, counts, inputs, groups, scale):
    size = CH * groups
    feeds = feed_slot.shape[0]
    wide = words.shape[2]
    bank = jnp.asarray(filter_bank())
    held = [jax.ShapeDtypeStruct((size, 2 * count, inputs), jnp.bfloat16) for count in counts]
    memory = pl.BlockSpec(memory_space=pltpu.VMEM)
    anywhere = pl.BlockSpec(memory_space=pl.ANY)
    chunks = len(counts)
    return pl.pallas_call(
        functools.partial(exchange_kernel, counts, groups, scale),
        out_shape=(held[-1], jax.ShapeDtypeStruct((2, ROWS, feeds), jnp.float32)),
        in_specs=[memory, anywhere, memory, memory, memory],
        out_specs=(anywhere, anywhere),
        scratch_shapes=[pltpu.VMEM((count + TAPS - 1, CH, wide), jnp.int32) for count in counts]
        + [pltpu.VMEM((CH, 2 * count, inputs), jnp.bfloat16) for count in counts]
        + [pltpu.VMEM(one.shape, one.dtype) for one in held[:-1]]
        + [
            pltpu.VMEM(((SPAN + TAPS) * 2 * CH, wide), jnp.bfloat16),
            pltpu.VMEM((2, wide // LANES, SPAN * CH, LANES), jnp.float32),
            pltpu.VMEM((2, ROWS, feeds), jnp.float32),
            pltpu.VMEM((2, ROWS, 2 * max(counts)), jnp.bfloat16),
            pltpu.SemaphoreType.DMA((chunks,)),
            pltpu.SemaphoreType.DMA((chunks,)),
            pltpu.SemaphoreType.DMA,
            pltpu.SemaphoreType.DMA((chunks, size)),
            pltpu.SemaphoreType.DMA((chunks, size)),
        ],
        compiler_params=pltpu.CompilerParams(
            collective_id=0, has_side_effects=True, vmem_limit_bytes=60 * 2**20
        ),
    )(bank, words, gains, feed_slot[None], own[None])


def finish_kernel(scale, moved_ref, slot_ref, own_ref, total_ref, out_ref, left):
    @pl.when(pl.program_id(0) == 0)
    def _():
        set_left(left, moved_ref, own_ref[...], scale)

    ordered = pick(moved_ref, slot_ref[...]).astype(jnp.bfloat16)
    for part in range(2):
        product = jnp.dot(left[part], ordered, preferred_element_type=jnp.float32)
        out_ref[:, part, :] = product + total_ref[part]


def split_kernel(counts, scale, bank_ref, words_hbm, gains_ref, slot_ref, own_ref, *refs):
    chunks = len(counts)
    refs = list(refs)

    def take(count):
        taken = refs[:count]
        del refs[:count]
        return taken

    last_hbm, total_hbm = take(2)
    words_bufs = take(chunks)
    send_bufs = take(chunks)
    full_bufs = take(chunks - 1)
    half_bufs = take(chunks)
    give_bufs = take(chunks)
    take_bufs = take(chunks)
    lefts = take(chunks)
    mine, theirs, voltage, rows, total, left = take(6)
    word_sem, own_sem, total_sem, near_sems, cross_sems, row_sems, product_sems = refs
    targets = full_bufs + [last_hbm]
    me = lax.axis_index("feed")
    size = lax.axis_size("feed")
    half = size // 2
    core = me % 2
    base = me // half * half
    away = half - base
    spot = me - base
    mate = away + spot + 1 - 2 * core
    quarter = me // (size // 4)
    inner = (quarter + 1) // 2 % 2
    inputs = send_bufs[0].shape[2]
    bank = bank_ref[...]
    gain = gains_ref[...].astype(jnp.float32) * (1.0 / 2048.0)

    barrier = pltpu.get_barrier_semaphore()

    def greet(d, carry):
        pl.semaphore_signal(
            barrier, inc=1, device_id={"feed": (me + d) % size}, device_id_type=pl.DeviceIdType.MESH
        )
        return carry

    lax.fori_loop(1, size, greet, 0)

    def loop(first, last, step):
        def one(i, carry):
            step(i)
            return carry

        lax.fori_loop(first, last, one, 0)

    def word_copy(k):
        source = words_hbm.at[pl.ds(sum(counts[:k]), counts[k] + TAPS - 1)]
        return pltpu.make_async_copy(source, words_bufs[k], word_sem.at[k])

    def remote(source, target, sems, place, there):
        send_sem, recv_sem = sems
        return pltpu.make_async_remote_copy(
            src_ref=source,
            dst_ref=target,
            send_sem=send_sem.at[place],
            recv_sem=recv_sem.at[place],
            device_id={"feed": there},
            device_id_type=pl.DeviceIdType.MESH,
        )

    def channel(place):
        odd = place % 2
        return (base + place) * (1 - odd) + (away + place - 1) * odd

    def near(k, d):
        place = (spot + d) % half
        return remote(
            send_bufs[k].at[channel(place)], half_bufs[k].at[spot], near_sems, (k, d), base + place
        )

    def near_own(k):
        return pltpu.make_async_copy(send_bufs[k].at[channel(spot)], half_bufs[k].at[spot], own_sem.at[0, k])

    def far(k, i):
        there = away + (spot + i) % half
        return remote(send_bufs[k].at[there], targets[k].at[me], cross_sems, (k, half + i), there)

    def close(k, i):
        there = base + (spot + i) % half
        return remote(send_bufs[k].at[there], targets[k].at[me], cross_sems, (k, i), there)

    def cross_own(k):
        return pltpu.make_async_copy(send_bufs[k].at[me], targets[k].at[me], own_sem.at[1, k])

    def row_copy(k):
        return remote(give_bufs[k], take_bufs[k], row_sems, k, mate)

    def product_copy(j):
        return remote(mine.at[j], theirs.at[j], product_sems, j, mate)

    def send_near(k):
        loop(1, half, lambda d: near(k, d).start())
        near_own(k).start()

    def arrive_near(k):
        near_own(k).wait()
        loop(1, half, lambda d: near(k, d).wait_recv())

    plane = half // 2

    def straight(k, q):
        return far(k, (q * plane + spot % plane // 2 * 2 + 1 - spot + half) % half)

    def across(k, q):
        return far(k, (q * plane + (spot + 2) % plane // 2 * 2 + 1 - spot + half) % half)

    def send_straight(k):
        loop(0, 2, lambda q: straight(k, q).start())

    def send_across(k):
        loop(0, 2, lambda q: across(k, q).start())

    def send_close(k):
        loop(core, half // 2, lambda q: close(k, 2 * q + 1 - core).start())

    senders = {"straight": send_straight, "across": send_across, "close": send_close}

    def issue(stage):
        for place, plan in ISSUE.items():
            steps = [step for step in plan if step[0] == stage]
            if steps:

                @pl.when((inner == place // 2) & (core == place % 2))
                def _(steps=steps):
                    for _, kind, k in steps:
                        senders[kind](k)

    def drain(k):
        loop(1, half, lambda d: near(k, d).wait_send())
        loop(0, half // 2, lambda q: far(k, 2 * q + 1 - core).wait_send())
        loop(core, half // 2, lambda q: close(k, 2 * q + 1 - core).wait_send())
        row_copy(k).wait_send()

    def arrive_cross(k):
        cross_own(k).start()
        cross_own(k).wait()
        loop(1, half, lambda i: close(k, i).wait_recv())
        loop(0, half, lambda i: far(k, i).wait_recv())

    for k in range(chunks):
        word_copy(k).start()
    for k in range(chunks):
        word_copy(k).wait()
        channelize(counts[k], bank, gain, words_bufs[k], send_bufs[k], voltage, rows)
        if k == 0:
            pl.semaphore_wait(barrier, size - 1)
        send_near(k)
        issue(k)

    for k in range(chunks):
        arrive_near(k)
        give_bufs[k][...] = pick(half_bufs[k], own_ref[...], base * inputs).astype(jnp.bfloat16)
        row_copy(k).start()

    issue(ROWS_SENT)

    for k in range(chunks):
        row_copy(k).wait_recv()
        both = give_bufs[k][...].astype(jnp.float32) + take_bufs[k][...].astype(jnp.float32)
        put_left(lefts[k], both, scale)

    def multiply(j):
        for part in range(2):
            product = None
            for k in range(chunks):
                term = jnp.dot(lefts[k][part], half_bufs[k][j], preferred_element_type=jnp.float32)
                product = term if product is None else product + term
            mine[j, part * ROWS : (part + 1) * ROWS, :] = product.astype(jnp.bfloat16)

        @pl.when(core == 1)
        def _():
            product_copy(j).start()

    loop(0, half, multiply)

    issue(PRODUCTS_SENT)

    feeds = slot_ref.shape[1]
    tile = min(TILE, feeds)

    @pl.when(core == 0)
    def _():
        def place_mine(j):
            where = pl.ds(pl.multiple_of(j * tile, tile), tile)
            ordered = pick(mine, slot_ref[:, where], base * inputs)
            total[0, :, where] = ordered[:ROWS]
            total[1, :, where] = ordered[ROWS:]

        def place_theirs(j):
            where = pl.ds(pl.multiple_of(j * tile, tile), tile)
            ordered = pick(theirs, slot_ref[:, where], away * inputs)
            total[0, :, where] = total[0, :, where] + ordered[:ROWS]
            total[1, :, where] = total[1, :, where] + ordered[ROWS:]

        loop(0, feeds // tile, place_mine)
        loop(0, half, lambda j: product_copy(j).wait_recv())
        loop(0, feeds // tile, place_theirs)

    @pl.when(core == 1)
    def _():
        for k in range(chunks - 1):
            arrive_cross(k)
            depth = 2 * counts[k]
            set_left(left, full_bufs[k], own_ref[...], scale)

            def columns(j, k=k, depth=depth):
                where = pl.ds(pl.multiple_of(j * tile, tile), tile)
                ordered = pick(full_bufs[k], slot_ref[:, where]).astype(jnp.bfloat16)
                for part in range(2):
                    product = jnp.dot(left[part, :, :depth], ordered, preferred_element_type=jnp.float32)
                    if k:
                        product = product + total[part, :, where]
                    total[part, :, where] = product

            loop(0, feeds // tile, columns)

    total_copy = pltpu.make_async_copy(total, total_hbm, total_sem)
    total_copy.start()

    @pl.when(core == 1)
    def _():
        arrive_cross(chunks - 1)
        loop(0, half, lambda j: product_copy(j).wait_send())

    for k in range(chunks):
        drain(k)
    total_copy.wait()


def split_exchange(words, gains, feed_slot, own, counts, inputs, scale):
    size = CH
    half = size // 2
    feeds = feed_slot.shape[0]
    wide = words.shape[2]
    bank = jnp.asarray(filter_bank())
    memory = pl.BlockSpec(memory_space=pltpu.VMEM)
    anywhere = pl.BlockSpec(memory_space=pl.ANY)
    chunks = len(counts)
    half_type = jnp.bfloat16
    return pl.pallas_call(
        functools.partial(split_kernel, counts, scale),
        out_shape=(
            jax.ShapeDtypeStruct((size, 2 * counts[-1], inputs), jnp.bfloat16),
            jax.ShapeDtypeStruct((2, ROWS, feeds), jnp.float32),
        ),
        in_specs=[memory, anywhere, memory, memory, memory],
        out_specs=(anywhere, anywhere),
        scratch_shapes=[pltpu.VMEM((count + TAPS - 1, CH, wide), jnp.int32) for count in counts]
        + [pltpu.VMEM((CH, 2 * count, inputs), half_type) for count in counts]
        + [pltpu.VMEM((size, 2 * count, inputs), half_type) for count in counts[:-1]]
        + [pltpu.VMEM((half, 2 * count, inputs), half_type) for count in counts]
        + [pltpu.VMEM((2 * count, ROWS), half_type) for count in counts] * 2
        + [pltpu.VMEM((2, ROWS, 2 * count), half_type) for count in counts]
        + [
            pltpu.VMEM((half, 2 * ROWS, inputs), half_type),
            pltpu.VMEM((half, 2 * ROWS, inputs), half_type),
            pltpu.VMEM(((SPAN + TAPS) * 2 * CH, wide), half_type),
            pltpu.VMEM((2, wide // LANES, SPAN * CH, LANES), jnp.float32),
            pltpu.VMEM((2, ROWS, feeds), jnp.float32),
            pltpu.VMEM((2, ROWS, 2 * max(counts)), half_type),
            pltpu.SemaphoreType.DMA((chunks,)),
            pltpu.SemaphoreType.DMA((2, chunks)),
            pltpu.SemaphoreType.DMA,
            (pltpu.SemaphoreType.DMA((chunks, half)),) * 2,
            (pltpu.SemaphoreType.DMA((chunks, size)),) * 2,
            (pltpu.SemaphoreType.DMA((chunks,)),) * 2,
            (pltpu.SemaphoreType.DMA((half,)),) * 2,
        ],
        compiler_params=pltpu.CompilerParams(
            collective_id=0, has_side_effects=True, vmem_limit_bytes=60 * 2**20
        ),
    )(bank, words, gains, feed_slot[None], own[None])


def split_finish_kernel(scale, moved_ref, slot_ref, own_ref, total_ref, out_ref, left):
    core = lax.axis_index("feed") % 2

    @pl.when(core == 0)
    def _():
        for part in range(2):
            out_ref[:, part, :] = total_ref[part]

    @pl.when(core == 1)
    def _():
        finish_kernel(scale, moved_ref, slot_ref, own_ref, total_ref, out_ref, left)


def finish(kernel, moved, feed_slot, own, total, scale):
    feeds = feed_slot.shape[0]
    tile = min(TILE, feeds)
    return pl.pallas_call(
        functools.partial(kernel, scale),
        out_shape=jax.ShapeDtypeStruct((ROWS, 2, feeds), jnp.float32),
        grid=(feeds // tile,),
        in_specs=[
            pl.BlockSpec(moved.shape, lambda j: (0, 0, 0)),
            pl.BlockSpec((1, tile), lambda j: (0, j)),
            pl.BlockSpec((1, ROWS), lambda j: (0, 0)),
            pl.BlockSpec((2, ROWS, tile), lambda j: (0, 0, j)),
        ],
        out_specs=pl.BlockSpec((ROWS, 2, tile), lambda j: (0, 0, j)),
        scratch_shapes=[pltpu.VMEM((2, ROWS, moved.shape[1]), jnp.bfloat16)],
    )(moved, feed_slot[None], own[None], total)


def body(samples, gains, feed_slot):
    groups = lax.axis_size("feed") // CH
    first = lax.axis_index("feed") % groups * ROWS
    inputs = samples.shape[0]
    spectra = samples.shape[2] - TAPS + 1
    split = groups == 1 and inputs % LANES == 0
    shares = SPLIT_SHARES if split else SHARES
    counts = tuple(spectra * share // sum(shares) for share in shares)
    words = jnp.transpose(samples, (2, 1, 0))
    spare = -inputs % LANES
    if spare:
        words = jnp.pad(words, ((0, 0), (0, 0), (0, spare)))
        gains = jnp.pad(gains, ((0, 0), (0, 0), (0, spare)))
    own = lax.dynamic_slice_in_dim(feed_slot, first, ROWS, 0)
    scale = 1.0 / spectra
    if split:
        moved, total = split_exchange(words, gains, feed_slot, own, counts, inputs, scale)
        return finish(split_finish_kernel, moved, feed_slot, own, total, scale)
    moved, total = exchange(words, gains, feed_slot, own, counts, inputs, groups, scale)
    return finish(finish_kernel, moved, feed_slot, own, total, scale)


def solution(mesh):
    return jax.shard_map(
        body,
        mesh=mesh,
        in_specs=(P(("band", "feed"), None, None), P(None, "band", "feed"), P()),
        out_specs=P(("band", "feed"), None, None),
        check_vma=False,
    )
```

```python
import functools
import math

import jax
import jax.numpy as jnp
import numpy as np
from jax import lax
from jax.experimental import pallas as pl
from jax.experimental.pallas import tpu as pltpu
from jax.sharding import PartitionSpec as P

CH = 16
TAPS = 8
SPECTRA = 512
ROWS = 256
SHARES = (4, 5, 5, 2)
SPLIT_SHARES = (1, 3, 2, 2)
SPAN = 32
TILE = 512
TERMS = 3
LANES = 128
FINISH_TILE = 1024
UNROLL = 32
ROWS_SENT, PRODUCTS_SENT, PRODUCTS_HERE = 100, 101, 102


def issue_plan():
    kinds = ("straight", "across", "close")
    chunks = range(len(SPLIT_SHARES))
    last = chunks[-1]
    plan = {}
    for core in range(2):
        inner = [(k, "straight", k) for k in chunks] + [(last, "across", k) for k in chunks]
        inner += [(PRODUCTS_SENT if core else ROWS_SENT, "close", k) for k in chunks]
        outer = []
        for k in chunks:
            stage = last if k < 2 - core else PRODUCTS_SENT if core else ROWS_SENT
            outer += [(stage, kind, k) for kind in kinds]
        plan[2 + core] = inner
        plan[core] = outer
    return plan


ISSUE = issue_plan()


def filter_bank():
    length = TAPS * CH
    place = np.arange(length, dtype=np.float64)
    window = 0.5 - 0.5 * np.cos(2.0 * math.pi * place / (length - 1))
    taps = (np.sinc((place - 0.5 * (length - 1)) / CH) * window).reshape(TAPS, CH)
    index = np.arange(CH)
    angle = (index[:, None] * index[None, :] % CH) * (2.0 * math.pi / CH)
    cosine = np.cos(angle) / math.sqrt(CH)
    sine = np.sin(angle) / math.sqrt(CH)
    table = np.stack([np.stack([cosine, sine], 1), np.stack([-sine, cosine], 1)], 0)
    bank = table[:, :, None, :, :] * taps[None, None, :, None, :]
    bank = 0.125 * bank.reshape(2 * CH, TAPS * 2 * CH)
    terms = []
    for _ in range(TERMS):
        term = bank.astype(jnp.bfloat16)
        terms.append(term)
        bank = bank - term.astype(np.float64)
    return np.concatenate(terms, 0)


def unpack(words):
    inphase = ((words >> 4) - 8).astype(jnp.float32).astype(jnp.bfloat16)
    quadrature = ((words & 15) - 8).astype(jnp.float32).astype(jnp.bfloat16)
    return jnp.concatenate([inphase, quadrature], axis=0)


def pick(moved_ref, columns, first=0):
    sources, _, width = moved_ref.shape
    total = None
    for source in range(sources):
        place = lax.broadcasted_iota(jnp.int32, (width, columns.shape[1]), 0) + (source * width + first)
        hot = jnp.where(place == columns, 1.0, 0.0).astype(jnp.bfloat16)
        part = jnp.dot(moved_ref[source], hot, preferred_element_type=jnp.float32)
        total = part if total is None else total + part
    return total


def put_left(left, picked, scale):
    depth = picked.shape[0]
    feed_rows = jnp.transpose(picked) * scale
    real, imag = feed_rows[:, : depth // 2], feed_rows[:, depth // 2 :]
    left[0, :, :depth] = jnp.concatenate([real, imag], axis=1).astype(jnp.bfloat16)
    left[1, :, :depth] = jnp.concatenate([imag, -real], axis=1).astype(jnp.bfloat16)


def set_left(left, moved_ref, columns, scale):
    put_left(left, pick(moved_ref, columns), scale)


def channelize(count, bank, gain, words, out, voltage, rows):
    inputs = out.shape[2]

    def block(i, carry):
        base = i * SPAN
        for m in range(SPAN + TAPS - 1):
            voltage[m * 2 * CH : (m + 1) * 2 * CH, :] = unpack(words[base + m])
        for s in range(SPAN):
            window = voltage[s * 2 * CH : (s + TAPS) * 2 * CH, :]
            parts = jnp.dot(bank, window, preferred_element_type=jnp.float32)
            whole = parts[: 2 * CH]
            for term in range(1, TERMS):
                whole = whole + parts[2 * CH * term : 2 * CH * (term + 1)]
            real, imag = whole[:CH], whole[CH:]
            upper = gain[0] * real - gain[1] * imag
            lower = gain[0] * imag + gain[1] * real
            for lane in range(rows.shape[1]):
                place = slice(lane * LANES, (lane + 1) * LANES)
                rows[0, lane, s * CH : (s + 1) * CH, :] = upper[:, place]
                rows[1, lane, s * CH : (s + 1) * CH, :] = lower[:, place]
        for c in range(CH):
            for part in range(2):
                where = pl.ds(pl.multiple_of(part * count + base, SPAN), SPAN)
                for lane in range(rows.shape[1]):
                    width = min(LANES, inputs - lane * LANES)
                    piece = rows[part, lane, pl.ds(c, SPAN, stride=CH), :]
                    out[c, where, lane * LANES : lane * LANES + width] = piece[:, :width].astype(
                        jnp.bfloat16
                    )
        return carry

    lax.fori_loop(0, count // SPAN, block, 0)


def exchange_kernel(counts, groups, scale, bank_ref, words_hbm, gains_ref, slot_ref, own_ref, *refs):
    chunks = len(counts)
    last_hbm, total_hbm = refs[:2]
    words_bufs = refs[2 : 2 + chunks]
    send_bufs = refs[2 + chunks : 2 + 2 * chunks]
    hold_bufs = refs[2 + 2 * chunks : 1 + 3 * chunks]
    voltage, rows, total, left, word_sem, own_sem, total_sem, send_sem, recv_sem = refs[1 + 3 * chunks :]
    targets = hold_bufs + (last_hbm,)
    me = lax.axis_index("feed")
    size = lax.axis_size("feed")
    bank = bank_ref[...]
    gain = gains_ref[...].astype(jnp.float32) * (1.0 / 2048.0)

    barrier = pltpu.get_barrier_semaphore()

    def greet(d, carry):
        pl.semaphore_signal(
            barrier, inc=1, device_id={"feed": (me + d) % size}, device_id_type=pl.DeviceIdType.MESH
        )
        return carry

    lax.fori_loop(1, size, greet, 0)

    def word_copy(k):
        source = words_hbm.at[pl.ds(sum(counts[:k]), counts[k] + TAPS - 1)]
        return pltpu.make_async_copy(source, words_bufs[k], word_sem.at[k])

    def own_copy(k):
        return pltpu.make_async_copy(send_bufs[k].at[me // groups], targets[k].at[me], own_sem.at[k])

    def remote(k, d):
        there = (me + d) % size
        return pltpu.make_async_remote_copy(
            src_ref=send_bufs[k].at[there // groups],
            dst_ref=targets[k].at[me],
            send_sem=send_sem.at[k, d],
            recv_sem=recv_sem.at[k, d],
            device_id={"feed": there},
            device_id_type=pl.DeviceIdType.MESH,
        )

    def send(k):
        def one(d, carry):
            remote(k, d).start()
            return carry

        lax.fori_loop(1, size, one, 0)
        own_copy(k).start()

    def arrive(k):
        def one(d, carry):
            remote(k, d).wait_recv()
            return carry

        own_copy(k).wait()
        lax.fori_loop(1, size, one, 0)

    def drain(k):
        def one(d, carry):
            remote(k, d).wait_send()
            return carry

        lax.fori_loop(1, size, one, 0)

    for k in range(chunks):
        word_copy(k).start()
    for k in range(chunks):
        word_copy(k).wait()
        channelize(counts[k], bank, gain, words_bufs[k], send_bufs[k], voltage, rows)
        if k == 0:
            pl.semaphore_wait(barrier, size - 1)
        send(k)

    feeds = slot_ref.shape[1]
    tile = min(TILE, feeds)
    for k in range(chunks - 1):
        arrive(k)
        depth = 2 * counts[k]
        set_left(left, hold_bufs[k], own_ref[...], scale)

        def columns(j, carry, k=k, depth=depth):
            where = pl.ds(pl.multiple_of(j * tile, tile), tile)
            ordered = pick(hold_bufs[k], slot_ref[:, where]).astype(jnp.bfloat16)
            for part in range(2):
                product = jnp.dot(left[part, :, :depth], ordered, preferred_element_type=jnp.float32)
                if k:
                    product = product + total[part, :, where]
                total[part, :, where] = product
            return carry

        lax.fori_loop(0, feeds // tile, columns, 0)
    total_copy = pltpu.make_async_copy(total, total_hbm, total_sem)
    total_copy.start()
    arrive(chunks - 1)
    for k in range(chunks):
        drain(k)
    total_copy.wait()


def exchange(words, gains, feed_slot, own, counts, inputs, groups, scale):
    size = CH * groups
    feeds = feed_slot.shape[0]
    wide = words.shape[2]
    bank = jnp.asarray(filter_bank())
    held = [jax.ShapeDtypeStruct((size, 2 * count, inputs), jnp.bfloat16) for count in counts]
    memory = pl.BlockSpec(memory_space=pltpu.VMEM)
    anywhere = pl.BlockSpec(memory_space=pl.ANY)
    chunks = len(counts)
    return pl.pallas_call(
        functools.partial(exchange_kernel, counts, groups, scale),
        out_shape=(held[-1], jax.ShapeDtypeStruct((2, ROWS, feeds), jnp.float32)),
        in_specs=[memory, anywhere, memory, memory, memory],
        out_specs=(anywhere, anywhere),
        scratch_shapes=[pltpu.VMEM((count + TAPS - 1, CH, wide), jnp.int32) for count in counts]
        + [pltpu.VMEM((CH, 2 * count, inputs), jnp.bfloat16) for count in counts]
        + [pltpu.VMEM(one.shape, one.dtype) for one in held[:-1]]
        + [
            pltpu.VMEM(((SPAN + TAPS) * 2 * CH, wide), jnp.bfloat16),
            pltpu.VMEM((2, wide // LANES, SPAN * CH, LANES), jnp.float32),
            pltpu.VMEM((2, ROWS, feeds), jnp.float32),
            pltpu.VMEM((2, ROWS, 2 * max(counts)), jnp.bfloat16),
            pltpu.SemaphoreType.DMA((chunks,)),
            pltpu.SemaphoreType.DMA((chunks,)),
            pltpu.SemaphoreType.DMA,
            pltpu.SemaphoreType.DMA((chunks, size)),
            pltpu.SemaphoreType.DMA((chunks, size)),
        ],
        compiler_params=pltpu.CompilerParams(
            collective_id=0, has_side_effects=True, vmem_limit_bytes=60 * 2**20
        ),
    )(bank, words, gains, feed_slot[None], own[None])


def finish_kernel(scale, moved_ref, slot_ref, own_ref, total_ref, out_ref, left):
    @pl.when(pl.program_id(0) == 0)
    def _():
        set_left(left, moved_ref, own_ref[...], scale)

    ordered = pick(moved_ref, slot_ref[...]).astype(jnp.bfloat16)
    for part in range(2):
        product = jnp.dot(left[part], ordered, preferred_element_type=jnp.float32)
        out_ref[:, part, :] = product + total_ref[part]


def split_kernel(counts, scale, bank_ref, words_hbm, gains_ref, own_ref, *refs):
    chunks = len(counts)
    refs = list(refs)

    def take(count):
        taken = refs[:count]
        del refs[:count]
        return taken

    (raw_hbm,) = take(1)
    words_bufs = take(chunks)
    send_bufs = take(chunks)
    full_bufs = take(chunks)
    half_bufs = take(chunks)
    give_bufs = take(chunks)
    take_bufs = take(chunks)
    lefts = take(chunks)
    mine, given, voltage, rows, total, left = take(6)
    word_sem, own_sem, raw_sem, near_sems, cross_sems, row_sems, product_sems = refs
    me = lax.axis_index("feed")
    size = lax.axis_size("feed")
    half = size // 2
    core = me % 2
    base = me // half * half
    away = half - base
    spot = me - base
    mate = away + spot + 1 - 2 * core
    quarter = me // (size // 4)
    inner = (quarter + 1) // 2 % 2
    inputs = send_bufs[0].shape[2]
    bank = bank_ref[...]
    gain = gains_ref[...].astype(jnp.float32) * (1.0 / 2048.0)

    barrier = pltpu.get_barrier_semaphore()

    def greet(d, carry):
        pl.semaphore_signal(
            barrier, inc=1, device_id={"feed": (me + d) % size}, device_id_type=pl.DeviceIdType.MESH
        )
        return carry

    lax.fori_loop(1, size, greet, 0)

    def loop(first, last, step):
        def one(i, carry):
            step(i)
            return carry

        lax.fori_loop(first, last, one, 0)

    def word_copy(k):
        source = words_hbm.at[pl.ds(sum(counts[:k]), counts[k] + TAPS - 1)]
        return pltpu.make_async_copy(source, words_bufs[k], word_sem.at[k])

    def remote(source, target, sems, place, there):
        send_sem, recv_sem = sems
        return pltpu.make_async_remote_copy(
            src_ref=source,
            dst_ref=target,
            send_sem=send_sem.at[place],
            recv_sem=recv_sem.at[place],
            device_id={"feed": there},
            device_id_type=pl.DeviceIdType.MESH,
        )

    def channel(place):
        odd = place % 2
        return (base + place) * (1 - odd) + (away + place - 1) * odd

    def near(k, d):
        place = (spot + d) % half
        return remote(
            send_bufs[k].at[channel(place)], half_bufs[k].at[spot], near_sems, (k, d), base + place
        )

    def near_own(k):
        return pltpu.make_async_copy(send_bufs[k].at[channel(spot)], half_bufs[k].at[spot], own_sem.at[0, k])

    def far(k, i):
        there = away + (spot + i) % half
        return remote(send_bufs[k].at[there], full_bufs[k].at[me], cross_sems, (k, half + i), there)

    def close(k, i):
        there = base + (spot + i) % half
        return remote(send_bufs[k].at[there], full_bufs[k].at[me], cross_sems, (k, i), there)

    def cross_own(k):
        return pltpu.make_async_copy(send_bufs[k].at[me], full_bufs[k].at[me], own_sem.at[1, k])

    def row_copy(k):
        return remote(give_bufs[k], take_bufs[k], row_sems, k, mate)

    def product_copy(j):
        return remote(given.at[j], raw_hbm.at[base + j], product_sems, j, mate)

    def send_near(k):
        loop(1, half, lambda d: near(k, d).start())
        near_own(k).start()

    def arrive_near(k):
        near_own(k).wait()
        loop(1, half, lambda d: near(k, d).wait_recv())

    plane = half // 2

    def straight(k, q):
        return far(k, (q * plane + spot % plane // 2 * 2 + 1 - spot + half) % half)

    def across(k, q):
        return far(k, (q * plane + (spot + 2) % plane // 2 * 2 + 1 - spot + half) % half)

    def send_straight(k):
        loop(0, 2, lambda q: straight(k, q).start())

    def send_across(k):
        loop(0, 2, lambda q: across(k, q).start())

    def send_close(k):
        loop(core, half // 2, lambda q: close(k, 2 * q + 1 - core).start())

    senders = {"straight": send_straight, "across": send_across, "close": send_close}

    def issue(stage):
        for place, plan in ISSUE.items():
            steps = [step for step in plan if step[0] == stage]
            if steps:

                @pl.when((inner == place // 2) & (core == place % 2))
                def _(steps=steps):
                    for _, kind, k in steps:
                        senders[kind](k)

    def drain(k):
        loop(1, half, lambda d: near(k, d).wait_send())
        loop(0, half // 2, lambda q: far(k, 2 * q + 1 - core).wait_send())
        loop(core, half // 2, lambda q: close(k, 2 * q + 1 - core).wait_send())
        row_copy(k).wait_send()

    def arrive_cross(k):
        cross_own(k).start()
        cross_own(k).wait()
        loop(1, half, lambda i: close(k, i).wait_recv())
        loop(0, half, lambda i: far(k, i).wait_recv())

    for k in range(chunks):
        word_copy(k).start()
    for k in range(chunks):
        word_copy(k).wait()
        channelize(counts[k], bank, gain, words_bufs[k], send_bufs[k], voltage, rows)
        if k == 0:
            pl.semaphore_wait(barrier, size - 1)
        send_near(k)
        issue(k)

    for k in range(chunks):
        arrive_near(k)
        give_bufs[k][...] = pick(half_bufs[k], own_ref[...], base * inputs).astype(jnp.bfloat16)
        row_copy(k).start()

    issue(ROWS_SENT)

    for k in range(chunks):
        row_copy(k).wait_recv()
        both = give_bufs[k][...].astype(jnp.float32) + take_bufs[k][...].astype(jnp.float32)
        put_left(lefts[k], both, scale)

    def raw_copy(buf, j, slot):
        return pltpu.make_async_copy(buf.at[slot], raw_hbm.at[j], raw_sem.at[j])

    def multiply(j):
        for part in range(2):
            product = None
            for k in range(chunks):
                term = jnp.dot(lefts[k][part], half_bufs[k][j], preferred_element_type=jnp.float32)
                product = term if product is None else product + term
            given[j, part * ROWS : (part + 1) * ROWS, :] = product.astype(jnp.bfloat16)

        @pl.when(core == 0)
        def _():
            raw_copy(given, base + j, j).start()

        @pl.when(core == 1)
        def _():
            product_copy(j).start()

    loop(0, half, multiply)
    issue(PRODUCTS_SENT)

    @pl.when(core == 0)
    def _():
        loop(0, half, lambda j: raw_copy(given, base + j, j).wait())
        loop(0, half, lambda j: product_copy(j).wait_recv())
        issue(PRODUCTS_HERE)

    @pl.when(core == 1)
    def _():
        for k in range(chunks):
            arrive_cross(k)
            depth = 2 * counts[k]
            set_left(left, full_bufs[k], own_ref[...], scale)

            def block(j, k=k, depth=depth):
                for part in range(2):
                    rows = slice(part * ROWS, (part + 1) * ROWS)
                    product = jnp.dot(left[part, :, :depth], full_bufs[k][j], preferred_element_type=jnp.float32)
                    if k:
                        product = product + total[j, rows, :]
                    if k < chunks - 1:
                        total[j, rows, :] = product
                    else:
                        mine[j, rows, :] = product.astype(jnp.bfloat16)
                if k == chunks - 1:
                    raw_copy(mine, j, j).start()

            loop(0, size, block)
        loop(0, size, lambda j: raw_copy(mine, j, j).wait())
        loop(0, half, lambda j: product_copy(j).wait_send())

    for k in range(chunks):
        drain(k)


def split_exchange(words, gains, own, counts, inputs, scale):
    size = CH
    half = size // 2
    wide = words.shape[2]
    bank = jnp.asarray(filter_bank())
    memory = pl.BlockSpec(memory_space=pltpu.VMEM)
    anywhere = pl.BlockSpec(memory_space=pl.ANY)
    chunks = len(counts)
    half_type = jnp.bfloat16
    return pl.pallas_call(
        functools.partial(split_kernel, counts, scale),
        out_shape=jax.ShapeDtypeStruct((size, 2 * ROWS, inputs), half_type),
        in_specs=[memory, anywhere, memory, memory],
        out_specs=anywhere,
        scratch_shapes=[pltpu.VMEM((count + TAPS - 1, CH, wide), jnp.int32) for count in counts]
        + [pltpu.VMEM((CH, 2 * count, inputs), half_type) for count in counts]
        + [pltpu.VMEM((size, 2 * count, inputs), half_type) for count in counts]
        + [pltpu.VMEM((half, 2 * count, inputs), half_type) for count in counts]
        + [pltpu.VMEM((2 * count, ROWS), half_type) for count in counts] * 2
        + [pltpu.VMEM((2, ROWS, 2 * count), half_type) for count in counts]
        + [
            pltpu.VMEM((size, 2 * ROWS, inputs), half_type),
            pltpu.VMEM((half, 2 * ROWS, inputs), half_type),
            pltpu.VMEM(((SPAN + TAPS) * 2 * CH, wide), half_type),
            pltpu.VMEM((2, wide // LANES, SPAN * CH, LANES), jnp.float32),
            pltpu.VMEM((size, 2 * ROWS, inputs), jnp.float32),
            pltpu.VMEM((2, ROWS, 2 * max(counts)), half_type),
            pltpu.SemaphoreType.DMA((chunks,)),
            pltpu.SemaphoreType.DMA((2, chunks)),
            pltpu.SemaphoreType.DMA((size,)),
            (pltpu.SemaphoreType.DMA((chunks, half)),) * 2,
            (pltpu.SemaphoreType.DMA((chunks, size)),) * 2,
            (pltpu.SemaphoreType.DMA((chunks,)),) * 2,
            (pltpu.SemaphoreType.DMA((half,)),) * 2,
        ],
        compiler_params=pltpu.CompilerParams(
            collective_id=0, has_side_effects=True, vmem_limit_bytes=60 * 2**20
        ),
    )(bank, words, gains, own[None])


def turn(block):
    size = block.shape[1]
    down = lax.broadcasted_iota(jnp.int32, (size, size), 0)
    along = lax.broadcasted_iota(jnp.int32, (size, size), 1)
    same = jnp.where(down == along, 1.0, 0.0).astype(jnp.bfloat16)
    return lax.dot_general(same, block, (((1,), (1,)), ((), ())), preferred_element_type=jnp.float32)


def split_finish_kernel(raw_ref, slot_ref, out_ref, table, picked):
    sources, depth, width = raw_ref.shape
    pieces = depth // LANES
    tile = out_ref.shape[2]
    first = pl.program_id(0) * tile

    @pl.when(pl.program_id(0) == 0)
    def _():
        def fill(source, carry):
            turned = turn(raw_ref[source])
            for piece in range(pieces):
                where = pl.ds(source * width * pieces + piece, width, stride=pieces)
                table[where, :] = turned[:, piece * LANES : (piece + 1) * LANES]
            return carry

        lax.fori_loop(0, sources, fill, 0)

    def gather(i, carry):
        for u in range(UNROLL):
            place = i * UNROLL + u
            slot = slot_ref[0, first + place]
            row = table[pl.ds(pl.multiple_of(slot * pieces, pieces), pieces), :]
            picked[pl.ds(pl.multiple_of(place * pieces, pieces), pieces), :] = row
        return carry

    lax.fori_loop(0, tile // UNROLL, gather, 0)
    per = ROWS // LANES
    for part in range(2):
        rows = [picked[pl.ds(part * per + piece, tile, stride=pieces), :] for piece in range(per)]
        out_ref[:, part, :] = turn(jnp.concatenate(rows, axis=1).astype(jnp.bfloat16))


def split_finish(raw, feed_slot):
    sources, depth, width = raw.shape
    feeds = feed_slot.shape[0]
    tile = min(FINISH_TILE, feeds)
    pieces = depth // LANES
    return pl.pallas_call(
        split_finish_kernel,
        out_shape=jax.ShapeDtypeStruct((ROWS, 2, feeds), jnp.float32),
        grid=(feeds // tile,),
        in_specs=[
            pl.BlockSpec(raw.shape, lambda j: (0, 0, 0), pipeline_mode=pl.Buffered(1)),
            pl.BlockSpec(memory_space=pltpu.SMEM),
        ],
        out_specs=pl.BlockSpec((ROWS, 2, tile), lambda j: (0, 0, j)),
        scratch_shapes=[
            pltpu.VMEM((sources * width * pieces, LANES), jnp.float32),
            pltpu.VMEM((tile * pieces, LANES), jnp.float32),
        ],
    )(raw, feed_slot[None])


def finish(moved, feed_slot, own, total, scale):
    feeds = feed_slot.shape[0]
    tile = min(TILE, feeds)
    return pl.pallas_call(
        functools.partial(finish_kernel, scale),
        out_shape=jax.ShapeDtypeStruct((ROWS, 2, feeds), jnp.float32),
        grid=(feeds // tile,),
        in_specs=[
            pl.BlockSpec(moved.shape, lambda j: (0, 0, 0)),
            pl.BlockSpec((1, tile), lambda j: (0, j)),
            pl.BlockSpec((1, ROWS), lambda j: (0, 0)),
            pl.BlockSpec((2, ROWS, tile), lambda j: (0, 0, j)),
        ],
        out_specs=pl.BlockSpec((ROWS, 2, tile), lambda j: (0, 0, j)),
        scratch_shapes=[pltpu.VMEM((2, ROWS, moved.shape[1]), jnp.bfloat16)],
    )(moved, feed_slot[None], own[None], total)


def body(samples, gains, feed_slot):
    groups = lax.axis_size("feed") // CH
    first = lax.axis_index("feed") % groups * ROWS
    inputs = samples.shape[0]
    spectra = samples.shape[2] - TAPS + 1
    split = groups == 1 and inputs % LANES == 0
    shares = SPLIT_SHARES if split else SHARES
    counts = tuple(spectra * share // sum(shares) for share in shares)
    words = jnp.transpose(samples, (2, 1, 0))
    spare = -inputs % LANES
    if spare:
        words = jnp.pad(words, ((0, 0), (0, 0), (0, spare)))
        gains = jnp.pad(gains, ((0, 0), (0, 0), (0, spare)))
    own = lax.dynamic_slice_in_dim(feed_slot, first, ROWS, 0)
    scale = 1.0 / spectra
    if split:
        raw = split_exchange(words, gains, own, counts, inputs, scale)
        return split_finish(raw, feed_slot)
    moved, total = exchange(words, gains, feed_slot, own, counts, inputs, groups, scale)
    return finish(moved, feed_slot, own, total, scale)


def solution(mesh):
    return jax.shard_map(
        body,
        mesh=mesh,
        in_specs=(P(("band", "feed"), None, None), P(None, "band", "feed"), P()),
        out_specs=P(("band", "feed"), None, None),
        check_vma=False,
    )
```

```python
import functools
import math

import jax
import jax.numpy as jnp
import numpy as np
from jax import lax
from jax.experimental import pallas as pl
from jax.experimental.pallas import tpu as pltpu
from jax.sharding import PartitionSpec as P

CH = 16
TAPS = 8
SPECTRA = 512
ROWS = 256
SHARES = (4, 5, 5, 2)
SPLIT_SHARES = (1, 3, 2, 2)
SPAN = 32
TILE = 512
TERMS = 3
LANES = 128
FINISH_TILE = 1024
STEP = 256
ROWS_SENT, PRODUCTS_SENT, PRODUCTS_HERE, ROW_STAGE = 100, 101, 102, 200


def issue_plan():
    kinds = ("straight", "across", "close")
    chunks = range(len(SPLIT_SHARES))
    last = chunks[-1]
    plan = {}
    for core in range(2):
        inner = [(k, "straight", k) for k in chunks] + [(last, "across", k) for k in chunks]
        inner += [(PRODUCTS_SENT if core else ROWS_SENT, "close", k) for k in chunks]
        outer = []
        for k in chunks:
            stage = ROW_STAGE + k if k < 2 - core else PRODUCTS_SENT if core else ROWS_SENT
            outer += [(stage, kind, k) for kind in kinds]
        plan[2 + core] = inner
        plan[core] = outer
    return plan


ISSUE = issue_plan()


def filter_bank():
    length = TAPS * CH
    place = np.arange(length, dtype=np.float64)
    window = 0.5 - 0.5 * np.cos(2.0 * math.pi * place / (length - 1))
    taps = (np.sinc((place - 0.5 * (length - 1)) / CH) * window).reshape(TAPS, CH)
    index = np.arange(CH)
    angle = (index[:, None] * index[None, :] % CH) * (2.0 * math.pi / CH)
    cosine = np.cos(angle) / math.sqrt(CH)
    sine = np.sin(angle) / math.sqrt(CH)
    table = np.stack([np.stack([cosine, sine], 1), np.stack([-sine, cosine], 1)], 0)
    bank = table[:, :, None, :, :] * taps[None, None, :, None, :]
    bank = 0.125 * bank.reshape(2 * CH, TAPS * 2 * CH)
    terms = []
    for _ in range(TERMS):
        term = bank.astype(jnp.bfloat16)
        terms.append(term)
        bank = bank - term.astype(np.float64)
    return np.concatenate(terms, 0)


def unpack(words):
    inphase = ((words >> 4) - 8).astype(jnp.float32).astype(jnp.bfloat16)
    quadrature = ((words & 15) - 8).astype(jnp.float32).astype(jnp.bfloat16)
    return jnp.concatenate([inphase, quadrature], axis=0)


def pick(moved_ref, columns, first=0):
    sources, _, width = moved_ref.shape
    total = None
    for source in range(sources):
        place = lax.broadcasted_iota(jnp.int32, (width, columns.shape[1]), 0) + (source * width + first)
        hot = jnp.where(place == columns, 1.0, 0.0).astype(jnp.bfloat16)
        part = jnp.dot(moved_ref[source], hot, preferred_element_type=jnp.float32)
        total = part if total is None else total + part
    return total


def put_left(left, picked, scale):
    depth = picked.shape[0]
    feed_rows = jnp.transpose(picked) * scale
    real, imag = feed_rows[:, : depth // 2], feed_rows[:, depth // 2 :]
    left[0, :, :depth] = jnp.concatenate([real, imag], axis=1).astype(jnp.bfloat16)
    left[1, :, :depth] = jnp.concatenate([imag, -real], axis=1).astype(jnp.bfloat16)


def set_left(left, moved_ref, columns, scale):
    put_left(left, pick(moved_ref, columns), scale)


def channelize(count, bank, gain, words, out, voltage, rows):
    inputs = out.shape[2]

    def block(i, carry):
        base = i * SPAN
        for m in range(SPAN + TAPS - 1):
            voltage[m * 2 * CH : (m + 1) * 2 * CH, :] = unpack(words[base + m])
        for s in range(SPAN):
            window = voltage[s * 2 * CH : (s + TAPS) * 2 * CH, :]
            parts = jnp.dot(bank, window, preferred_element_type=jnp.float32)
            whole = parts[: 2 * CH]
            for term in range(1, TERMS):
                whole = whole + parts[2 * CH * term : 2 * CH * (term + 1)]
            real, imag = whole[:CH], whole[CH:]
            upper = gain[0] * real - gain[1] * imag
            lower = gain[0] * imag + gain[1] * real
            for lane in range(rows.shape[1]):
                place = slice(lane * LANES, (lane + 1) * LANES)
                rows[0, lane, s * CH : (s + 1) * CH, :] = upper[:, place]
                rows[1, lane, s * CH : (s + 1) * CH, :] = lower[:, place]
        for c in range(CH):
            for part in range(2):
                where = pl.ds(pl.multiple_of(part * count + base, SPAN), SPAN)
                for lane in range(rows.shape[1]):
                    width = min(LANES, inputs - lane * LANES)
                    piece = rows[part, lane, pl.ds(c, SPAN, stride=CH), :]
                    out[c, where, lane * LANES : lane * LANES + width] = piece[:, :width].astype(
                        jnp.bfloat16
                    )
        return carry

    lax.fori_loop(0, count // SPAN, block, 0)


def exchange_kernel(counts, groups, scale, bank_ref, words_hbm, gains_ref, slot_ref, own_ref, *refs):
    chunks = len(counts)
    last_hbm, total_hbm = refs[:2]
    words_bufs = refs[2 : 2 + chunks]
    send_bufs = refs[2 + chunks : 2 + 2 * chunks]
    hold_bufs = refs[2 + 2 * chunks : 1 + 3 * chunks]
    voltage, rows, total, left, word_sem, own_sem, total_sem, send_sem, recv_sem = refs[1 + 3 * chunks :]
    targets = hold_bufs + (last_hbm,)
    me = lax.axis_index("feed")
    size = lax.axis_size("feed")
    bank = bank_ref[...]
    gain = gains_ref[...].astype(jnp.float32) * (1.0 / 2048.0)

    barrier = pltpu.get_barrier_semaphore()

    def greet(d, carry):
        pl.semaphore_signal(
            barrier, inc=1, device_id={"feed": (me + d) % size}, device_id_type=pl.DeviceIdType.MESH
        )
        return carry

    lax.fori_loop(1, size, greet, 0)

    def word_copy(k):
        source = words_hbm.at[pl.ds(sum(counts[:k]), counts[k] + TAPS - 1)]
        return pltpu.make_async_copy(source, words_bufs[k], word_sem.at[k])

    def own_copy(k):
        return pltpu.make_async_copy(send_bufs[k].at[me // groups], targets[k].at[me], own_sem.at[k])

    def remote(k, d):
        there = (me + d) % size
        return pltpu.make_async_remote_copy(
            src_ref=send_bufs[k].at[there // groups],
            dst_ref=targets[k].at[me],
            send_sem=send_sem.at[k, d],
            recv_sem=recv_sem.at[k, d],
            device_id={"feed": there},
            device_id_type=pl.DeviceIdType.MESH,
        )

    def send(k):
        def one(d, carry):
            remote(k, d).start()
            return carry

        lax.fori_loop(1, size, one, 0)
        own_copy(k).start()

    def arrive(k):
        def one(d, carry):
            remote(k, d).wait_recv()
            return carry

        own_copy(k).wait()
        lax.fori_loop(1, size, one, 0)

    def drain(k):
        def one(d, carry):
            remote(k, d).wait_send()
            return carry

        lax.fori_loop(1, size, one, 0)

    for k in range(chunks):
        word_copy(k).start()
    for k in range(chunks):
        word_copy(k).wait()
        channelize(counts[k], bank, gain, words_bufs[k], send_bufs[k], voltage, rows)
        if k == 0:
            pl.semaphore_wait(barrier, size - 1)
        send(k)

    feeds = slot_ref.shape[1]
    tile = min(TILE, feeds)
    for k in range(chunks - 1):
        arrive(k)
        depth = 2 * counts[k]
        set_left(left, hold_bufs[k], own_ref[...], scale)

        def columns(j, carry, k=k, depth=depth):
            where = pl.ds(pl.multiple_of(j * tile, tile), tile)
            ordered = pick(hold_bufs[k], slot_ref[:, where]).astype(jnp.bfloat16)
            for part in range(2):
                product = jnp.dot(left[part, :, :depth], ordered, preferred_element_type=jnp.float32)
                if k:
                    product = product + total[part, :, where]
                total[part, :, where] = product
            return carry

        lax.fori_loop(0, feeds // tile, columns, 0)
    total_copy = pltpu.make_async_copy(total, total_hbm, total_sem)
    total_copy.start()
    arrive(chunks - 1)
    for k in range(chunks):
        drain(k)
    total_copy.wait()


def exchange(words, gains, feed_slot, own, counts, inputs, groups, scale):
    size = CH * groups
    feeds = feed_slot.shape[0]
    wide = words.shape[2]
    bank = jnp.asarray(filter_bank())
    held = [jax.ShapeDtypeStruct((size, 2 * count, inputs), jnp.bfloat16) for count in counts]
    memory = pl.BlockSpec(memory_space=pltpu.VMEM)
    anywhere = pl.BlockSpec(memory_space=pl.ANY)
    chunks = len(counts)
    return pl.pallas_call(
        functools.partial(exchange_kernel, counts, groups, scale),
        out_shape=(held[-1], jax.ShapeDtypeStruct((2, ROWS, feeds), jnp.float32)),
        in_specs=[memory, anywhere, memory, memory, memory],
        out_specs=(anywhere, anywhere),
        scratch_shapes=[pltpu.VMEM((count + TAPS - 1, CH, wide), jnp.int32) for count in counts]
        + [pltpu.VMEM((CH, 2 * count, inputs), jnp.bfloat16) for count in counts]
        + [pltpu.VMEM(one.shape, one.dtype) for one in held[:-1]]
        + [
            pltpu.VMEM(((SPAN + TAPS) * 2 * CH, wide), jnp.bfloat16),
            pltpu.VMEM((2, wide // LANES, SPAN * CH, LANES), jnp.float32),
            pltpu.VMEM((2, ROWS, feeds), jnp.float32),
            pltpu.VMEM((2, ROWS, 2 * max(counts)), jnp.bfloat16),
            pltpu.SemaphoreType.DMA((chunks,)),
            pltpu.SemaphoreType.DMA((chunks,)),
            pltpu.SemaphoreType.DMA,
            pltpu.SemaphoreType.DMA((chunks, size)),
            pltpu.SemaphoreType.DMA((chunks, size)),
        ],
        compiler_params=pltpu.CompilerParams(
            collective_id=0, has_side_effects=True, vmem_limit_bytes=60 * 2**20
        ),
    )(bank, words, gains, feed_slot[None], own[None])


def finish_kernel(scale, moved_ref, slot_ref, own_ref, total_ref, out_ref, left):
    @pl.when(pl.program_id(0) == 0)
    def _():
        set_left(left, moved_ref, own_ref[...], scale)

    ordered = pick(moved_ref, slot_ref[...]).astype(jnp.bfloat16)
    for part in range(2):
        product = jnp.dot(left[part], ordered, preferred_element_type=jnp.float32)
        out_ref[:, part, :] = product + total_ref[part]


def split_kernel(counts, scale, bank_ref, words_hbm, gains_ref, slot_ref, *refs):
    chunks = len(counts)
    refs = list(refs)

    def take(count):
        taken = refs[:count]
        del refs[:count]
        return taken

    (raw_hbm,) = take(1)
    words_bufs = take(chunks)
    send_bufs = take(chunks)
    full_bufs = take(chunks)
    half_bufs = take(chunks)
    give_bufs = take(chunks)
    take_bufs = take(chunks)
    lefts = take(chunks)
    mine, given, voltage, rows, total, left = take(6)
    word_sem, own_sem, raw_sem, near_sems, cross_sems, row_sems, product_sems = refs
    me = lax.axis_index("feed")
    size = lax.axis_size("feed")
    half = size // 2
    core = me % 2
    base = me // half * half
    away = half - base
    spot = me - base
    mate = away + spot + 1 - 2 * core
    quarter = me // (size // 4)
    inner = (quarter + 1) // 2 % 2
    inputs = send_bufs[0].shape[2]
    bank = bank_ref[...]
    own = slot_ref[:, :ROWS]
    gain = gains_ref[...].astype(jnp.float32) * (1.0 / 2048.0)

    barrier = pltpu.get_barrier_semaphore()

    def greet(d, carry):
        pl.semaphore_signal(
            barrier, inc=1, device_id={"feed": (me + d) % size}, device_id_type=pl.DeviceIdType.MESH
        )
        return carry

    lax.fori_loop(1, size, greet, 0)

    def loop(first, last, step):
        def one(i, carry):
            step(i)
            return carry

        lax.fori_loop(first, last, one, 0)

    def word_copy(k):
        source = words_hbm.at[pl.ds(sum(counts[:k]), counts[k] + TAPS - 1)]
        return pltpu.make_async_copy(source, words_bufs[k], word_sem.at[k])

    def remote(source, target, sems, place, there):
        send_sem, recv_sem = sems
        return pltpu.make_async_remote_copy(
            src_ref=source,
            dst_ref=target,
            send_sem=send_sem.at[place],
            recv_sem=recv_sem.at[place],
            device_id={"feed": there},
            device_id_type=pl.DeviceIdType.MESH,
        )

    def channel(place):
        odd = place % 2
        return (base + place) * (1 - odd) + (away + place - 1) * odd

    def near(k, d):
        place = (spot + d) % half
        return remote(
            send_bufs[k].at[channel(place)], half_bufs[k].at[spot], near_sems, (k, d), base + place
        )

    def near_own(k):
        return pltpu.make_async_copy(send_bufs[k].at[channel(spot)], half_bufs[k].at[spot], own_sem.at[0, k])

    def far(k, i):
        there = away + (spot + i) % half
        return remote(send_bufs[k].at[there], full_bufs[k].at[me], cross_sems, (k, half + i), there)

    def close(k, i):
        there = base + (spot + i) % half
        return remote(send_bufs[k].at[there], full_bufs[k].at[me], cross_sems, (k, i), there)

    def cross_own(k):
        return pltpu.make_async_copy(send_bufs[k].at[me], full_bufs[k].at[me], own_sem.at[1, k])

    def row_copy(k):
        return remote(give_bufs[k], take_bufs[k], row_sems, k, mate)

    def product_copy(j):
        return remote(given.at[j], raw_hbm.at[base + j], product_sems, j, mate)

    def send_near(k):
        loop(1, half, lambda d: near(k, d).start())
        near_own(k).start()

    def arrive_near(k):
        near_own(k).wait()
        loop(1, half, lambda d: near(k, d).wait_recv())

    plane = half // 2

    def straight(k, q):
        return far(k, (q * plane + spot % plane // 2 * 2 + 1 - spot + half) % half)

    def across(k, q):
        return far(k, (q * plane + (spot + 2) % plane // 2 * 2 + 1 - spot + half) % half)

    def send_straight(k):
        loop(0, 2, lambda q: straight(k, q).start())

    def send_across(k):
        loop(0, 2, lambda q: across(k, q).start())

    def send_close(k):
        loop(core, half // 2, lambda q: close(k, 2 * q + 1 - core).start())

    senders = {"straight": send_straight, "across": send_across, "close": send_close}

    def issue(stage):
        for place, plan in ISSUE.items():
            steps = [step for step in plan if step[0] == stage]
            if steps:

                @pl.when((inner == place // 2) & (core == place % 2))
                def _(steps=steps):
                    for _, kind, k in steps:
                        senders[kind](k)

    def drain(k):
        loop(1, half, lambda d: near(k, d).wait_send())
        loop(0, half // 2, lambda q: far(k, 2 * q + 1 - core).wait_send())
        loop(core, half // 2, lambda q: close(k, 2 * q + 1 - core).wait_send())
        row_copy(k).wait_send()

    def arrive_cross(k):
        cross_own(k).start()
        cross_own(k).wait()
        loop(1, half, lambda i: close(k, i).wait_recv())
        loop(0, half, lambda i: far(k, i).wait_recv())

    for k in range(chunks):
        word_copy(k).start()
    for k in range(chunks):
        word_copy(k).wait()
        channelize(counts[k], bank, gain, words_bufs[k], send_bufs[k], voltage, rows)
        if k == 0:
            pl.semaphore_wait(barrier, size - 1)
        send_near(k)
        issue(k)

    for k in range(chunks):
        arrive_near(k)
        give_bufs[k][...] = pick(half_bufs[k], own, base * inputs).astype(jnp.bfloat16)
        row_copy(k).start()
        issue(ROW_STAGE + k)

    issue(ROWS_SENT)

    for k in range(chunks):
        row_copy(k).wait_recv()
        both = give_bufs[k][...].astype(jnp.float32) + take_bufs[k][...].astype(jnp.float32)
        put_left(lefts[k], both, scale)

    def raw_copy(buf, j, slot):
        return pltpu.make_async_copy(buf.at[slot], raw_hbm.at[j], raw_sem.at[j])

    def multiply(j):
        for part in range(2):
            product = None
            for k in range(chunks):
                term = jnp.dot(lefts[k][part], half_bufs[k][j], preferred_element_type=jnp.float32)
                product = term if product is None else product + term
            given[j, part * ROWS : (part + 1) * ROWS, :] = product.astype(jnp.bfloat16)

        @pl.when(core == 0)
        def _():
            raw_copy(given, base + j, j).start()

        @pl.when(core == 1)
        def _():
            product_copy(j).start()

    loop(0, half, multiply)
    issue(PRODUCTS_SENT)

    @pl.when(core == 0)
    def _():
        loop(0, half, lambda j: raw_copy(given, base + j, j).wait())
        loop(0, half, lambda j: product_copy(j).wait_recv())
        issue(PRODUCTS_HERE)

    @pl.when(core == 1)
    def _():
        for k in range(chunks):
            arrive_cross(k)
            depth = 2 * counts[k]
            set_left(left, full_bufs[k], own, scale)

            def block(j, k=k, depth=depth):
                for part in range(2):
                    rows = slice(part * ROWS, (part + 1) * ROWS)
                    product = jnp.dot(left[part, :, :depth], full_bufs[k][j], preferred_element_type=jnp.float32)
                    if k:
                        product = product + total[j, rows, :]
                    if k < chunks - 1:
                        total[j, rows, :] = product
                    else:
                        mine[j, rows, :] = product.astype(jnp.bfloat16)
                if k == chunks - 1:
                    raw_copy(mine, j, j).start()

            loop(0, size, block)
        loop(0, size, lambda j: raw_copy(mine, j, j).wait())
        loop(0, half, lambda j: product_copy(j).wait_send())

    for k in range(chunks):
        drain(k)


def split_exchange(words, gains, feed_slot, counts, inputs, scale):
    size = CH
    half = size // 2
    wide = words.shape[2]
    bank = jnp.asarray(filter_bank())
    memory = pl.BlockSpec(memory_space=pltpu.VMEM)
    anywhere = pl.BlockSpec(memory_space=pl.ANY)
    chunks = len(counts)
    half_type = jnp.bfloat16
    return pl.pallas_call(
        functools.partial(split_kernel, counts, scale),
        out_shape=jax.ShapeDtypeStruct((size, 2 * ROWS, inputs), half_type),
        in_specs=[memory, anywhere, memory, memory],
        out_specs=anywhere,
        scratch_shapes=[pltpu.VMEM((count + TAPS - 1, CH, wide), jnp.int32) for count in counts]
        + [pltpu.VMEM((CH, 2 * count, inputs), half_type) for count in counts]
        + [pltpu.VMEM((size, 2 * count, inputs), half_type) for count in counts]
        + [pltpu.VMEM((half, 2 * count, inputs), half_type) for count in counts]
        + [pltpu.VMEM((2 * count, ROWS), half_type) for count in counts] * 2
        + [pltpu.VMEM((2, ROWS, 2 * count), half_type) for count in counts]
        + [
            pltpu.VMEM((size, 2 * ROWS, inputs), half_type),
            pltpu.VMEM((half, 2 * ROWS, inputs), half_type),
            pltpu.VMEM(((SPAN + TAPS) * 2 * CH, wide), half_type),
            pltpu.VMEM((2, wide // LANES, SPAN * CH, LANES), jnp.float32),
            pltpu.VMEM((size, 2 * ROWS, inputs), jnp.float32),
            pltpu.VMEM((2, ROWS, 2 * max(counts)), half_type),
            pltpu.SemaphoreType.DMA((chunks,)),
            pltpu.SemaphoreType.DMA((2, chunks)),
            pltpu.SemaphoreType.DMA((size,)),
            (pltpu.SemaphoreType.DMA((chunks, half)),) * 2,
            (pltpu.SemaphoreType.DMA((chunks, size)),) * 2,
            (pltpu.SemaphoreType.DMA((chunks,)),) * 2,
            (pltpu.SemaphoreType.DMA((half,)),) * 2,
        ],
        compiler_params=pltpu.CompilerParams(
            collective_id=0, has_side_effects=True, vmem_limit_bytes=60 * 2**20
        ),
    )(bank, words, gains, feed_slot[None])


def turn(block):
    size = block.shape[1]
    down = lax.broadcasted_iota(jnp.int32, (size, size), 0)
    along = lax.broadcasted_iota(jnp.int32, (size, size), 1)
    same = jnp.where(down == along, 1.0, 0.0).astype(jnp.bfloat16)
    return lax.dot_general(same, block, (((1,), (1,)), ((), ())), preferred_element_type=jnp.float32)


def split_finish_kernel(raw_hbm, slot_ref, out_ref, raw, table, even, odd, sems):
    sources, depth, width = raw.shape
    pieces = depth // LANES
    per = ROWS // LANES
    tile = out_ref.shape[2]
    first = pl.program_id(0) * tile
    step = even.shape[0] // pieces

    def raw_copy(source):
        return pltpu.make_async_copy(raw_hbm.at[source], raw.at[source], sems.at[source])

    @pl.when(pl.program_id(0) == 0)
    def _():
        def begin(source, carry):
            raw_copy(source).start()
            return carry

        def fill(source, carry):
            raw_copy(source).wait()
            turned = turn(raw[source])
            for piece in range(pieces):
                where = pl.ds(source * width * pieces + piece, width, stride=pieces)
                table[where, :] = turned[:, piece * LANES : (piece + 1) * LANES]
            return carry

        lax.fori_loop(0, sources, begin, 0)
        lax.fori_loop(0, sources, fill, 0)

    def gather(picked, begin):
        for place in range(step):
            slot = slot_ref[0, first + begin + place]
            row = table[pl.ds(pl.multiple_of(slot * pieces, pieces), pieces), :]
            picked[place * pieces : (place + 1) * pieces, :] = row

    def put(picked, begin):
        for part in range(2):
            rows = [picked[pl.ds(part * per + piece, step, stride=pieces), :] for piece in range(per)]
            turned = turn(jnp.concatenate(rows, axis=1).astype(jnp.bfloat16))
            out_ref[:, part, begin : begin + step] = turned

    gather(even, 0)
    for i in range(tile // step):
        here, there = (even, odd) if i % 2 == 0 else (odd, even)
        if i + 1 < tile // step:
            gather(there, (i + 1) * step)
        put(here, i * step)


def split_finish(raw, feed_slot):
    sources, depth, width = raw.shape
    feeds = feed_slot.shape[0]
    tile = min(FINISH_TILE, feeds)
    step = min(STEP, tile)
    pieces = depth // LANES
    return pl.pallas_call(
        split_finish_kernel,
        out_shape=jax.ShapeDtypeStruct((ROWS, 2, feeds), jnp.float32),
        grid=(feeds // tile,),
        in_specs=[pl.BlockSpec(memory_space=pl.ANY), pl.BlockSpec(memory_space=pltpu.SMEM)],
        out_specs=pl.BlockSpec((ROWS, 2, tile), lambda j: (0, 0, j)),
        scratch_shapes=[
            pltpu.VMEM(raw.shape, raw.dtype),
            pltpu.VMEM((sources * width * pieces, LANES), jnp.float32),
            pltpu.VMEM((step * pieces, LANES), jnp.float32),
            pltpu.VMEM((step * pieces, LANES), jnp.float32),
            pltpu.SemaphoreType.DMA((sources,)),
        ],
    )(raw, feed_slot[None])


def finish(moved, feed_slot, own, total, scale):
    feeds = feed_slot.shape[0]
    tile = min(TILE, feeds)
    return pl.pallas_call(
        functools.partial(finish_kernel, scale),
        out_shape=jax.ShapeDtypeStruct((ROWS, 2, feeds), jnp.float32),
        grid=(feeds // tile,),
        in_specs=[
            pl.BlockSpec(moved.shape, lambda j: (0, 0, 0)),
            pl.BlockSpec((1, tile), lambda j: (0, j)),
            pl.BlockSpec((1, ROWS), lambda j: (0, 0)),
            pl.BlockSpec((2, ROWS, tile), lambda j: (0, 0, j)),
        ],
        out_specs=pl.BlockSpec((ROWS, 2, tile), lambda j: (0, 0, j)),
        scratch_shapes=[pltpu.VMEM((2, ROWS, moved.shape[1]), jnp.bfloat16)],
    )(moved, feed_slot[None], own[None], total)


def body(samples, gains, feed_slot):
    groups = lax.axis_size("feed") // CH
    first = lax.axis_index("feed") % groups * ROWS
    inputs = samples.shape[0]
    spectra = samples.shape[2] - TAPS + 1
    split = groups == 1 and inputs % LANES == 0
    shares = SPLIT_SHARES if split else SHARES
    counts = tuple(spectra * share // sum(shares) for share in shares)
    words = jnp.transpose(samples, (2, 1, 0))
    spare = -inputs % LANES
    if spare:
        words = jnp.pad(words, ((0, 0), (0, 0), (0, spare)))
        gains = jnp.pad(gains, ((0, 0), (0, 0), (0, spare)))
    scale = 1.0 / spectra
    if split:
        raw = split_exchange(words, gains, feed_slot, counts, inputs, scale)
        return split_finish(raw, feed_slot)
    own = lax.dynamic_slice_in_dim(feed_slot, first, ROWS, 0)
    moved, total = exchange(words, gains, feed_slot, own, counts, inputs, groups, scale)
    return finish(moved, feed_slot, own, total, scale)


def solution(mesh):
    return jax.shard_map(
        body,
        mesh=mesh,
        in_specs=(P(("band", "feed"), None, None), P(None, "band", "feed"), P()),
        out_specs=P(("band", "feed"), None, None),
        check_vma=False,
    )
```

```python
import functools
import math

import jax
import jax.numpy as jnp
import numpy as np
from jax import lax
from jax.experimental import pallas as pl
from jax.experimental.pallas import tpu as pltpu
from jax.sharding import PartitionSpec as P

CH = 16
TAPS = 8
SPECTRA = 512
ROWS = 256
SHARES = (4, 5, 5, 2)
SPLIT_SHARES = (1, 3, 2, 2)
SPAN = 32
TILE = 512
TERMS = 3
LANES = 128
FINISH_TILE = 1024
STEP = 512
ROWS_SENT, PRODUCTS_SENT, PRODUCTS_HERE, ROW_STAGE = 100, 101, 102, 200


def issue_plan():
    kinds = ("straight", "across", "close")
    chunks = range(len(SPLIT_SHARES))
    last = chunks[-1]
    plan = {}
    for core in range(2):
        inner = [(k, "straight", k) for k in chunks] + [(last, "across", k) for k in chunks]
        inner += [(PRODUCTS_SENT if core else ROWS_SENT, "close", k) for k in chunks]
        outer = []
        for k in chunks:
            stage = ROW_STAGE + k if k < 2 - core else PRODUCTS_SENT if core else ROWS_SENT
            outer += [(stage, kind, k) for kind in kinds]
        plan[2 + core] = inner
        plan[core] = outer
    return plan


ISSUE = issue_plan()


def filter_bank():
    length = TAPS * CH
    place = np.arange(length, dtype=np.float64)
    window = 0.5 - 0.5 * np.cos(2.0 * math.pi * place / (length - 1))
    taps = (np.sinc((place - 0.5 * (length - 1)) / CH) * window).reshape(TAPS, CH)
    index = np.arange(CH)
    angle = (index[:, None] * index[None, :] % CH) * (2.0 * math.pi / CH)
    cosine = np.cos(angle) / math.sqrt(CH)
    sine = np.sin(angle) / math.sqrt(CH)
    table = np.stack([np.stack([cosine, sine], 1), np.stack([-sine, cosine], 1)], 0)
    bank = table[:, :, None, :, :] * taps[None, None, :, None, :]
    bank = 0.125 * bank.reshape(2 * CH, TAPS * 2 * CH)
    terms = []
    for _ in range(TERMS):
        term = bank.astype(jnp.bfloat16)
        terms.append(term)
        bank = bank - term.astype(np.float64)
    return np.concatenate(terms, 0)


def unpack(words):
    inphase = ((words >> 4) - 8).astype(jnp.float32).astype(jnp.bfloat16)
    quadrature = ((words & 15) - 8).astype(jnp.float32).astype(jnp.bfloat16)
    return jnp.concatenate([inphase, quadrature], axis=0)


def pick(moved_ref, columns, first=0):
    sources, _, width = moved_ref.shape
    total = None
    for source in range(sources):
        place = lax.broadcasted_iota(jnp.int32, (width, columns.shape[1]), 0) + (source * width + first)
        hot = jnp.where(place == columns, 1.0, 0.0).astype(jnp.bfloat16)
        part = jnp.dot(moved_ref[source], hot, preferred_element_type=jnp.float32)
        total = part if total is None else total + part
    return total


def put_left(left, picked, scale):
    depth = picked.shape[0]
    feed_rows = jnp.transpose(picked) * scale
    real, imag = feed_rows[:, : depth // 2], feed_rows[:, depth // 2 :]
    left[0, :, :depth] = jnp.concatenate([real, imag], axis=1).astype(jnp.bfloat16)
    left[1, :, :depth] = jnp.concatenate([imag, -real], axis=1).astype(jnp.bfloat16)


def set_left(left, moved_ref, columns, scale):
    put_left(left, pick(moved_ref, columns), scale)


def channelize(count, bank, gain, words, out, voltage, rows):
    inputs = out.shape[2]

    def block(i, carry):
        base = i * SPAN
        for m in range(SPAN + TAPS - 1):
            voltage[m * 2 * CH : (m + 1) * 2 * CH, :] = unpack(words[base + m])
        for s in range(SPAN):
            window = voltage[s * 2 * CH : (s + TAPS) * 2 * CH, :]
            parts = jnp.dot(bank, window, preferred_element_type=jnp.float32)
            whole = parts[: 2 * CH]
            for term in range(1, TERMS):
                whole = whole + parts[2 * CH * term : 2 * CH * (term + 1)]
            real, imag = whole[:CH], whole[CH:]
            upper = gain[0] * real - gain[1] * imag
            lower = gain[0] * imag + gain[1] * real
            for lane in range(rows.shape[1]):
                place = slice(lane * LANES, (lane + 1) * LANES)
                rows[0, lane, s * CH : (s + 1) * CH, :] = upper[:, place]
                rows[1, lane, s * CH : (s + 1) * CH, :] = lower[:, place]
        for c in range(CH):
            for part in range(2):
                where = pl.ds(pl.multiple_of(part * count + base, SPAN), SPAN)
                for lane in range(rows.shape[1]):
                    width = min(LANES, inputs - lane * LANES)
                    piece = rows[part, lane, pl.ds(c, SPAN, stride=CH), :]
                    out[c, where, lane * LANES : lane * LANES + width] = piece[:, :width].astype(
                        jnp.bfloat16
                    )
        return carry

    lax.fori_loop(0, count // SPAN, block, 0)


def exchange_kernel(counts, groups, scale, bank_ref, words_hbm, gains_ref, slot_ref, own_ref, *refs):
    chunks = len(counts)
    last_hbm, total_hbm = refs[:2]
    words_bufs = refs[2 : 2 + chunks]
    send_bufs = refs[2 + chunks : 2 + 2 * chunks]
    hold_bufs = refs[2 + 2 * chunks : 1 + 3 * chunks]
    voltage, rows, total, left, word_sem, own_sem, total_sem, send_sem, recv_sem = refs[1 + 3 * chunks :]
    targets = hold_bufs + (last_hbm,)
    me = lax.axis_index("feed")
    size = lax.axis_size("feed")
    bank = bank_ref[...]
    gain = gains_ref[...].astype(jnp.float32) * (1.0 / 2048.0)

    barrier = pltpu.get_barrier_semaphore()

    def greet(d, carry):
        pl.semaphore_signal(
            barrier, inc=1, device_id={"feed": (me + d) % size}, device_id_type=pl.DeviceIdType.MESH
        )
        return carry

    lax.fori_loop(1, size, greet, 0)

    def word_copy(k):
        source = words_hbm.at[pl.ds(sum(counts[:k]), counts[k] + TAPS - 1)]
        return pltpu.make_async_copy(source, words_bufs[k], word_sem.at[k])

    def own_copy(k):
        return pltpu.make_async_copy(send_bufs[k].at[me // groups], targets[k].at[me], own_sem.at[k])

    def remote(k, d):
        there = (me + d) % size
        return pltpu.make_async_remote_copy(
            src_ref=send_bufs[k].at[there // groups],
            dst_ref=targets[k].at[me],
            send_sem=send_sem.at[k, d],
            recv_sem=recv_sem.at[k, d],
            device_id={"feed": there},
            device_id_type=pl.DeviceIdType.MESH,
        )

    def send(k):
        def one(d, carry):
            remote(k, d).start()
            return carry

        lax.fori_loop(1, size, one, 0)
        own_copy(k).start()

    def arrive(k):
        def one(d, carry):
            remote(k, d).wait_recv()
            return carry

        own_copy(k).wait()
        lax.fori_loop(1, size, one, 0)

    def drain(k):
        def one(d, carry):
            remote(k, d).wait_send()
            return carry

        lax.fori_loop(1, size, one, 0)

    for k in range(chunks):
        word_copy(k).start()
    for k in range(chunks):
        word_copy(k).wait()
        channelize(counts[k], bank, gain, words_bufs[k], send_bufs[k], voltage, rows)
        if k == 0:
            pl.semaphore_wait(barrier, size - 1)
        send(k)

    feeds = slot_ref.shape[1]
    tile = min(TILE, feeds)
    for k in range(chunks - 1):
        arrive(k)
        depth = 2 * counts[k]
        set_left(left, hold_bufs[k], own_ref[...], scale)

        def columns(j, carry, k=k, depth=depth):
            where = pl.ds(pl.multiple_of(j * tile, tile), tile)
            ordered = pick(hold_bufs[k], slot_ref[:, where]).astype(jnp.bfloat16)
            for part in range(2):
                product = jnp.dot(left[part, :, :depth], ordered, preferred_element_type=jnp.float32)
                if k:
                    product = product + total[part, :, where]
                total[part, :, where] = product
            return carry

        lax.fori_loop(0, feeds // tile, columns, 0)
    total_copy = pltpu.make_async_copy(total, total_hbm, total_sem)
    total_copy.start()
    arrive(chunks - 1)
    for k in range(chunks):
        drain(k)
    total_copy.wait()


def exchange(words, gains, feed_slot, own, counts, inputs, groups, scale):
    size = CH * groups
    feeds = feed_slot.shape[0]
    wide = words.shape[2]
    bank = jnp.asarray(filter_bank())
    held = [jax.ShapeDtypeStruct((size, 2 * count, inputs), jnp.bfloat16) for count in counts]
    memory = pl.BlockSpec(memory_space=pltpu.VMEM)
    anywhere = pl.BlockSpec(memory_space=pl.ANY)
    chunks = len(counts)
    return pl.pallas_call(
        functools.partial(exchange_kernel, counts, groups, scale),
        out_shape=(held[-1], jax.ShapeDtypeStruct((2, ROWS, feeds), jnp.float32)),
        in_specs=[memory, anywhere, memory, memory, memory],
        out_specs=(anywhere, anywhere),
        scratch_shapes=[pltpu.VMEM((count + TAPS - 1, CH, wide), jnp.int32) for count in counts]
        + [pltpu.VMEM((CH, 2 * count, inputs), jnp.bfloat16) for count in counts]
        + [pltpu.VMEM(one.shape, one.dtype) for one in held[:-1]]
        + [
            pltpu.VMEM(((SPAN + TAPS) * 2 * CH, wide), jnp.bfloat16),
            pltpu.VMEM((2, wide // LANES, SPAN * CH, LANES), jnp.float32),
            pltpu.VMEM((2, ROWS, feeds), jnp.float32),
            pltpu.VMEM((2, ROWS, 2 * max(counts)), jnp.bfloat16),
            pltpu.SemaphoreType.DMA((chunks,)),
            pltpu.SemaphoreType.DMA((chunks,)),
            pltpu.SemaphoreType.DMA,
            pltpu.SemaphoreType.DMA((chunks, size)),
            pltpu.SemaphoreType.DMA((chunks, size)),
        ],
        compiler_params=pltpu.CompilerParams(
            collective_id=0, has_side_effects=True, vmem_limit_bytes=60 * 2**20
        ),
    )(bank, words, gains, feed_slot[None], own[None])


def finish_kernel(scale, moved_ref, slot_ref, own_ref, total_ref, out_ref, left):
    @pl.when(pl.program_id(0) == 0)
    def _():
        set_left(left, moved_ref, own_ref[...], scale)

    ordered = pick(moved_ref, slot_ref[...]).astype(jnp.bfloat16)
    for part in range(2):
        product = jnp.dot(left[part], ordered, preferred_element_type=jnp.float32)
        out_ref[:, part, :] = product + total_ref[part]


def split_kernel(counts, scale, bank_ref, words_hbm, gains_ref, slot_ref, *refs):
    chunks = len(counts)
    refs = list(refs)

    def take(count):
        taken = refs[:count]
        del refs[:count]
        return taken

    (raw_hbm,) = take(1)
    words_bufs = take(chunks)
    send_bufs = take(chunks)
    full_bufs = take(chunks)
    half_bufs = take(chunks)
    give_bufs = take(chunks)
    take_bufs = take(chunks)
    lefts = take(chunks)
    mine, given, voltage, rows, total, left = take(6)
    word_sem, own_sem, raw_sem, near_sems, cross_sems, row_sems, product_sems = refs
    me = lax.axis_index("feed")
    size = lax.axis_size("feed")
    half = size // 2
    core = me % 2
    base = me // half * half
    away = half - base
    spot = me - base
    mate = away + spot + 1 - 2 * core
    quarter = me // (size // 4)
    inner = (quarter + 1) // 2 % 2
    inputs = send_bufs[0].shape[2]
    bank = bank_ref[...]
    own = slot_ref[:, :ROWS]
    gain = gains_ref[...].astype(jnp.float32) * (1.0 / 2048.0)

    barrier = pltpu.get_barrier_semaphore()

    def greet(d, carry):
        pl.semaphore_signal(
            barrier, inc=1, device_id={"feed": (me + d) % size}, device_id_type=pl.DeviceIdType.MESH
        )
        return carry

    lax.fori_loop(1, size, greet, 0)

    def loop(first, last, step):
        def one(i, carry):
            step(i)
            return carry

        lax.fori_loop(first, last, one, 0)

    def word_copy(k):
        source = words_hbm.at[pl.ds(sum(counts[:k]), counts[k] + TAPS - 1)]
        return pltpu.make_async_copy(source, words_bufs[k], word_sem.at[k])

    def remote(source, target, sems, place, there):
        send_sem, recv_sem = sems
        return pltpu.make_async_remote_copy(
            src_ref=source,
            dst_ref=target,
            send_sem=send_sem.at[place],
            recv_sem=recv_sem.at[place],
            device_id={"feed": there},
            device_id_type=pl.DeviceIdType.MESH,
        )

    def channel(place):
        odd = place % 2
        return (base + place) * (1 - odd) + (away + place - 1) * odd

    def near(k, d):
        place = (spot + d) % half
        return remote(
            send_bufs[k].at[channel(place)], half_bufs[k].at[spot], near_sems, (k, d), base + place
        )

    def near_own(k):
        return pltpu.make_async_copy(send_bufs[k].at[channel(spot)], half_bufs[k].at[spot], own_sem.at[0, k])

    def far(k, i):
        there = away + (spot + i) % half
        return remote(send_bufs[k].at[there], full_bufs[k].at[me], cross_sems, (k, half + i), there)

    def close(k, i):
        there = base + (spot + i) % half
        return remote(send_bufs[k].at[there], full_bufs[k].at[me], cross_sems, (k, i), there)

    def cross_own(k):
        return pltpu.make_async_copy(send_bufs[k].at[me], full_bufs[k].at[me], own_sem.at[1, k])

    def row_copy(k):
        return remote(give_bufs[k], take_bufs[k], row_sems, k, mate)

    def product_copy(j):
        return remote(given.at[j], raw_hbm.at[base + j], product_sems, j, mate)

    def send_near(k):
        loop(1, half, lambda d: near(k, d).start())
        near_own(k).start()

    def arrive_near(k):
        near_own(k).wait()
        loop(1, half, lambda d: near(k, d).wait_recv())

    plane = half // 2

    def straight(k, q):
        return far(k, (q * plane + spot % plane // 2 * 2 + 1 - spot + half) % half)

    def across(k, q):
        return far(k, (q * plane + (spot + 2) % plane // 2 * 2 + 1 - spot + half) % half)

    def send_straight(k):
        loop(0, 2, lambda q: straight(k, q).start())

    def send_across(k):
        loop(0, 2, lambda q: across(k, q).start())

    def send_close(k):
        loop(core, half // 2, lambda q: close(k, 2 * q + 1 - core).start())

    senders = {"straight": send_straight, "across": send_across, "close": send_close}

    def issue(stage):
        for place, plan in ISSUE.items():
            steps = [step for step in plan if step[0] == stage]
            if steps:

                @pl.when((inner == place // 2) & (core == place % 2))
                def _(steps=steps):
                    for _, kind, k in steps:
                        senders[kind](k)

    def drain(k):
        loop(1, half, lambda d: near(k, d).wait_send())
        loop(0, half // 2, lambda q: far(k, 2 * q + 1 - core).wait_send())
        loop(core, half // 2, lambda q: close(k, 2 * q + 1 - core).wait_send())
        row_copy(k).wait_send()

    def arrive_cross(k):
        cross_own(k).start()
        cross_own(k).wait()
        loop(1, half, lambda i: close(k, i).wait_recv())
        loop(0, half, lambda i: far(k, i).wait_recv())

    word_copy(0).start()
    for k in range(chunks):
        word_copy(k).wait()
        if k + 1 < chunks:
            word_copy(k + 1).start()
        channelize(counts[k], bank, gain, words_bufs[k], send_bufs[k], voltage, rows)
        if k == 0:
            pl.semaphore_wait(barrier, size - 1)
        send_near(k)
        issue(k)

    for k in range(chunks):
        arrive_near(k)
        give_bufs[k][...] = pick(half_bufs[k], own, base * inputs).astype(jnp.bfloat16)
        row_copy(k).start()
        issue(ROW_STAGE + k)

    issue(ROWS_SENT)

    for k in range(chunks):
        row_copy(k).wait_recv()
        both = give_bufs[k][...].astype(jnp.float32) + take_bufs[k][...].astype(jnp.float32)
        put_left(lefts[k], both, scale)

    def raw_copy(buf, j, slot):
        return pltpu.make_async_copy(buf.at[slot], raw_hbm.at[j], raw_sem.at[j])

    def multiply(j):
        for part in range(2):
            product = None
            for k in range(chunks):
                term = jnp.dot(lefts[k][part], half_bufs[k][j], preferred_element_type=jnp.float32)
                product = term if product is None else product + term
            given[j, part * ROWS : (part + 1) * ROWS, :] = product.astype(jnp.bfloat16)

        @pl.when(core == 0)
        def _():
            raw_copy(given, base + j, j).start()

        @pl.when(core == 1)
        def _():
            product_copy(j).start()

    loop(0, half, multiply)
    issue(PRODUCTS_SENT)

    @pl.when(core == 0)
    def _():
        loop(0, half, lambda j: raw_copy(given, base + j, j).wait())
        loop(0, half, lambda j: product_copy(j).wait_recv())
        issue(PRODUCTS_HERE)

    @pl.when(core == 1)
    def _():
        for k in range(chunks):
            arrive_cross(k)
            depth = 2 * counts[k]
            set_left(left, full_bufs[k], own, scale)

            def block(j, k=k, depth=depth):
                for part in range(2):
                    rows = slice(part * ROWS, (part + 1) * ROWS)
                    product = jnp.dot(left[part, :, :depth], full_bufs[k][j], preferred_element_type=jnp.float32)
                    if k:
                        product = product + total[j, rows, :]
                    if k < chunks - 1:
                        total[j, rows, :] = product
                    else:
                        mine[j, rows, :] = product.astype(jnp.bfloat16)
                if k == chunks - 1:
                    raw_copy(mine, j, j).start()

            loop(0, size, block)
        loop(0, size, lambda j: raw_copy(mine, j, j).wait())
        loop(0, half, lambda j: product_copy(j).wait_send())

    for k in range(chunks):
        drain(k)


def split_exchange(words, gains, feed_slot, counts, inputs, scale):
    size = CH
    half = size // 2
    wide = words.shape[2]
    bank = jnp.asarray(filter_bank())
    memory = pl.BlockSpec(memory_space=pltpu.VMEM)
    anywhere = pl.BlockSpec(memory_space=pl.ANY)
    chunks = len(counts)
    half_type = jnp.bfloat16
    return pl.pallas_call(
        functools.partial(split_kernel, counts, scale),
        out_shape=jax.ShapeDtypeStruct((size, 2 * ROWS, inputs), half_type),
        in_specs=[memory, anywhere, memory, memory],
        out_specs=anywhere,
        scratch_shapes=[pltpu.VMEM((count + TAPS - 1, CH, wide), jnp.int32) for count in counts]
        + [pltpu.VMEM((CH, 2 * count, inputs), half_type) for count in counts]
        + [pltpu.VMEM((size, 2 * count, inputs), half_type) for count in counts]
        + [pltpu.VMEM((half, 2 * count, inputs), half_type) for count in counts]
        + [pltpu.VMEM((2 * count, ROWS), half_type) for count in counts] * 2
        + [pltpu.VMEM((2, ROWS, 2 * count), half_type) for count in counts]
        + [
            pltpu.VMEM((size, 2 * ROWS, inputs), half_type),
            pltpu.VMEM((half, 2 * ROWS, inputs), half_type),
            pltpu.VMEM(((SPAN + TAPS) * 2 * CH, wide), half_type),
            pltpu.VMEM((2, wide // LANES, SPAN * CH, LANES), jnp.float32),
            pltpu.VMEM((size, 2 * ROWS, inputs), jnp.float32),
            pltpu.VMEM((2, ROWS, 2 * max(counts)), half_type),
            pltpu.SemaphoreType.DMA((chunks,)),
            pltpu.SemaphoreType.DMA((2, chunks)),
            pltpu.SemaphoreType.DMA((size,)),
            (pltpu.SemaphoreType.DMA((chunks, half)),) * 2,
            (pltpu.SemaphoreType.DMA((chunks, size)),) * 2,
            (pltpu.SemaphoreType.DMA((chunks,)),) * 2,
            (pltpu.SemaphoreType.DMA((half,)),) * 2,
        ],
        compiler_params=pltpu.CompilerParams(
            collective_id=0, has_side_effects=True, vmem_limit_bytes=60 * 2**20
        ),
    )(bank, words, gains, feed_slot[None])


def turn(block):
    size = block.shape[1]
    down = lax.broadcasted_iota(jnp.int32, (size, size), 0)
    along = lax.broadcasted_iota(jnp.int32, (size, size), 1)
    same = jnp.where(down == along, 1.0, 0.0).astype(jnp.bfloat16)
    return lax.dot_general(same, block, (((1,), (1,)), ((), ())), preferred_element_type=jnp.float32)


def split_finish_kernel(raw_hbm, slot_ref, out_ref, raw, table, even, odd, sems):
    sources, depth, width = raw.shape
    pieces = depth // LANES
    per = ROWS // LANES
    tile = out_ref.shape[2]
    first = pl.program_id(0) * tile
    step = even.shape[0] // pieces

    def raw_copy(source):
        return pltpu.make_async_copy(raw_hbm.at[source], raw.at[source], sems.at[source])

    @pl.when(pl.program_id(0) == 0)
    def _():
        def begin(source, carry):
            raw_copy(source).start()
            return carry

        def fill(source, carry):
            raw_copy(source).wait()
            turned = turn(raw[source])
            for piece in range(pieces):
                where = pl.ds(source * width * pieces + piece, width, stride=pieces)
                table[where, :] = turned[:, piece * LANES : (piece + 1) * LANES]
            return carry

        lax.fori_loop(0, sources, begin, 0)
        lax.fori_loop(0, sources, fill, 0)

    def gather(picked, begin):
        for place in range(step):
            slot = slot_ref[0, first + begin + place]
            row = table[pl.ds(pl.multiple_of(slot * pieces, pieces), pieces), :]
            picked[place * pieces : (place + 1) * pieces, :] = row

    def put(picked, begin):
        for part in range(2):
            rows = [picked[pl.ds(part * per + piece, step, stride=pieces), :] for piece in range(per)]
            turned = turn(jnp.concatenate(rows, axis=1).astype(jnp.bfloat16))
            out_ref[:, part, begin : begin + step] = turned

    gather(even, 0)
    for i in range(tile // step):
        here, there = (even, odd) if i % 2 == 0 else (odd, even)
        if i + 1 < tile // step:
            gather(there, (i + 1) * step)
        put(here, i * step)


def split_finish(raw, feed_slot):
    sources, depth, width = raw.shape
    feeds = feed_slot.shape[0]
    tile = min(FINISH_TILE, feeds)
    step = min(STEP, tile)
    pieces = depth // LANES
    return pl.pallas_call(
        split_finish_kernel,
        out_shape=jax.ShapeDtypeStruct((ROWS, 2, feeds), jnp.float32),
        grid=(feeds // tile,),
        in_specs=[pl.BlockSpec(memory_space=pl.ANY), pl.BlockSpec(memory_space=pltpu.SMEM)],
        out_specs=pl.BlockSpec((ROWS, 2, tile), lambda j: (0, 0, j)),
        scratch_shapes=[
            pltpu.VMEM(raw.shape, raw.dtype),
            pltpu.VMEM((sources * width * pieces, LANES), jnp.float32),
            pltpu.VMEM((step * pieces, LANES), jnp.float32),
            pltpu.VMEM((step * pieces, LANES), jnp.float32),
            pltpu.SemaphoreType.DMA((sources,)),
        ],
    )(raw, feed_slot[None])


def finish(moved, feed_slot, own, total, scale):
    feeds = feed_slot.shape[0]
    tile = min(TILE, feeds)
    return pl.pallas_call(
        functools.partial(finish_kernel, scale),
        out_shape=jax.ShapeDtypeStruct((ROWS, 2, feeds), jnp.float32),
        grid=(feeds // tile,),
        in_specs=[
            pl.BlockSpec(moved.shape, lambda j: (0, 0, 0)),
            pl.BlockSpec((1, tile), lambda j: (0, j)),
            pl.BlockSpec((1, ROWS), lambda j: (0, 0)),
            pl.BlockSpec((2, ROWS, tile), lambda j: (0, 0, j)),
        ],
        out_specs=pl.BlockSpec((ROWS, 2, tile), lambda j: (0, 0, j)),
        scratch_shapes=[pltpu.VMEM((2, ROWS, moved.shape[1]), jnp.bfloat16)],
    )(moved, feed_slot[None], own[None], total)


def body(samples, gains, feed_slot):
    groups = lax.axis_size("feed") // CH
    first = lax.axis_index("feed") % groups * ROWS
    inputs = samples.shape[0]
    spectra = samples.shape[2] - TAPS + 1
    split = groups == 1 and inputs % LANES == 0
    shares = SPLIT_SHARES if split else SHARES
    counts = tuple(spectra * share // sum(shares) for share in shares)
    words = jnp.transpose(samples, (2, 1, 0))
    spare = -inputs % LANES
    if spare:
        words = jnp.pad(words, ((0, 0), (0, 0), (0, spare)))
        gains = jnp.pad(gains, ((0, 0), (0, 0), (0, spare)))
    scale = 1.0 / spectra
    if split:
        raw = split_exchange(words, gains, feed_slot, counts, inputs, scale)
        return split_finish(raw, feed_slot)
    own = lax.dynamic_slice_in_dim(feed_slot, first, ROWS, 0)
    moved, total = exchange(words, gains, feed_slot, own, counts, inputs, groups, scale)
    return finish(moved, feed_slot, own, total, scale)


def solution(mesh):
    return jax.shard_map(
        body,
        mesh=mesh,
        in_specs=(P(("band", "feed"), None, None), P(None, "band", "feed"), P()),
        out_specs=P(("band", "feed"), None, None),
        check_vma=False,
    )
```

```python
import functools
import math

import jax
import jax.numpy as jnp
import numpy as np
from jax import lax
from jax.experimental import pallas as pl
from jax.experimental.pallas import tpu as pltpu
from jax.sharding import PartitionSpec as P

CH = 16
TAPS = 8
SPECTRA = 512
ROWS = 256
SHARES = (4, 5, 5, 2)
SPLIT_SHARES = (1, 3, 2, 2)
SPAN = 32
TILE = 512
TERMS = 3
LANES = 128
FINISH_TILE = 1024
STEP = 512
ROWS_SENT, PRODUCTS_SENT, PRODUCTS_HERE, ROW_STAGE = 100, 101, 102, 200


def issue_plan():
    kinds = ("across", "straight", "close")
    chunks = range(len(SPLIT_SHARES))
    last = chunks[-1]
    plan = {}
    for core in range(2):
        inner = [(k, "straight", k) for k in chunks] + [(last, "across", k) for k in chunks]
        inner += [(ROWS_SENT, "close", k) for k in chunks]
        outer = []
        for k in chunks:
            stage = ROW_STAGE + k if k < 2 - core else PRODUCTS_SENT if core else ROWS_SENT
            outer += [(stage, kind, k) for kind in kinds]
        plan[2 + core] = inner
        plan[core] = outer
    return plan


ISSUE = issue_plan()


def filter_bank():
    length = TAPS * CH
    place = np.arange(length, dtype=np.float64)
    window = 0.5 - 0.5 * np.cos(2.0 * math.pi * place / (length - 1))
    taps = (np.sinc((place - 0.5 * (length - 1)) / CH) * window).reshape(TAPS, CH)
    index = np.arange(CH)
    angle = (index[:, None] * index[None, :] % CH) * (2.0 * math.pi / CH)
    cosine = np.cos(angle) / math.sqrt(CH)
    sine = np.sin(angle) / math.sqrt(CH)
    table = np.stack([np.stack([cosine, sine], 1), np.stack([-sine, cosine], 1)], 0)
    bank = table[:, :, None, :, :] * taps[None, None, :, None, :]
    bank = 0.125 * bank.reshape(2 * CH, TAPS * 2 * CH)
    terms = []
    for _ in range(TERMS):
        term = bank.astype(jnp.bfloat16)
        terms.append(term)
        bank = bank - term.astype(np.float64)
    return np.concatenate(terms, 0)


def unpack(words):
    inphase = ((words >> 4) - 8).astype(jnp.float32).astype(jnp.bfloat16)
    quadrature = ((words & 15) - 8).astype(jnp.float32).astype(jnp.bfloat16)
    return jnp.concatenate([inphase, quadrature], axis=0)


def pick(moved_ref, columns, first=0):
    sources, _, width = moved_ref.shape
    total = None
    for source in range(sources):
        place = lax.broadcasted_iota(jnp.int32, (width, columns.shape[1]), 0) + (source * width + first)
        hot = jnp.where(place == columns, 1.0, 0.0).astype(jnp.bfloat16)
        part = jnp.dot(moved_ref[source], hot, preferred_element_type=jnp.float32)
        total = part if total is None else total + part
    return total


def put_left(left, picked, scale):
    depth = picked.shape[0]
    feed_rows = jnp.transpose(picked) * scale
    real, imag = feed_rows[:, : depth // 2], feed_rows[:, depth // 2 :]
    left[0, :, :depth] = jnp.concatenate([real, imag], axis=1).astype(jnp.bfloat16)
    left[1, :, :depth] = jnp.concatenate([imag, -real], axis=1).astype(jnp.bfloat16)


def set_left(left, moved_ref, columns, scale):
    put_left(left, pick(moved_ref, columns), scale)


def channelize(count, bank, gain, words, out, voltage, rows):
    inputs = out.shape[2]

    def block(i, carry):
        base = i * SPAN
        for m in range(SPAN + TAPS - 1):
            voltage[m * 2 * CH : (m + 1) * 2 * CH, :] = unpack(words[base + m])
        for s in range(SPAN):
            window = voltage[s * 2 * CH : (s + TAPS) * 2 * CH, :]
            parts = jnp.dot(bank, window, preferred_element_type=jnp.float32)
            whole = parts[: 2 * CH]
            for term in range(1, TERMS):
                whole = whole + parts[2 * CH * term : 2 * CH * (term + 1)]
            real, imag = whole[:CH], whole[CH:]
            upper = gain[0] * real - gain[1] * imag
            lower = gain[0] * imag + gain[1] * real
            for lane in range(rows.shape[1]):
                place = slice(lane * LANES, (lane + 1) * LANES)
                rows[0, lane, s * CH : (s + 1) * CH, :] = upper[:, place]
                rows[1, lane, s * CH : (s + 1) * CH, :] = lower[:, place]
        for c in range(CH):
            for part in range(2):
                where = pl.ds(pl.multiple_of(part * count + base, SPAN), SPAN)
                for lane in range(rows.shape[1]):
                    width = min(LANES, inputs - lane * LANES)
                    piece = rows[part, lane, pl.ds(c, SPAN, stride=CH), :]
                    out[c, where, lane * LANES : lane * LANES + width] = piece[:, :width].astype(
                        jnp.bfloat16
                    )
        return carry

    lax.fori_loop(0, count // SPAN, block, 0)


def exchange_kernel(counts, groups, scale, bank_ref, words_hbm, gains_ref, slot_ref, own_ref, *refs):
    chunks = len(counts)
    last_hbm, total_hbm = refs[:2]
    words_bufs = refs[2 : 2 + chunks]
    send_bufs = refs[2 + chunks : 2 + 2 * chunks]
    hold_bufs = refs[2 + 2 * chunks : 1 + 3 * chunks]
    voltage, rows, total, left, word_sem, own_sem, total_sem, send_sem, recv_sem = refs[1 + 3 * chunks :]
    targets = hold_bufs + (last_hbm,)
    me = lax.axis_index("feed")
    size = lax.axis_size("feed")
    bank = bank_ref[...]
    gain = gains_ref[...].astype(jnp.float32) * (1.0 / 2048.0)

    barrier = pltpu.get_barrier_semaphore()

    def greet(d, carry):
        pl.semaphore_signal(
            barrier, inc=1, device_id={"feed": (me + d) % size}, device_id_type=pl.DeviceIdType.MESH
        )
        return carry

    lax.fori_loop(1, size, greet, 0)

    def word_copy(k):
        source = words_hbm.at[pl.ds(sum(counts[:k]), counts[k] + TAPS - 1)]
        return pltpu.make_async_copy(source, words_bufs[k], word_sem.at[k])

    def own_copy(k):
        return pltpu.make_async_copy(send_bufs[k].at[me // groups], targets[k].at[me], own_sem.at[k])

    def remote(k, d):
        there = (me + d) % size
        return pltpu.make_async_remote_copy(
            src_ref=send_bufs[k].at[there // groups],
            dst_ref=targets[k].at[me],
            send_sem=send_sem.at[k, d],
            recv_sem=recv_sem.at[k, d],
            device_id={"feed": there},
            device_id_type=pl.DeviceIdType.MESH,
        )

    def send(k):
        def one(d, carry):
            remote(k, d).start()
            return carry

        lax.fori_loop(1, size, one, 0)
        own_copy(k).start()

    def arrive(k):
        def one(d, carry):
            remote(k, d).wait_recv()
            return carry

        own_copy(k).wait()
        lax.fori_loop(1, size, one, 0)

    def drain(k):
        def one(d, carry):
            remote(k, d).wait_send()
            return carry

        lax.fori_loop(1, size, one, 0)

    for k in range(chunks):
        word_copy(k).start()
    for k in range(chunks):
        word_copy(k).wait()
        channelize(counts[k], bank, gain, words_bufs[k], send_bufs[k], voltage, rows)
        if k == 0:
            pl.semaphore_wait(barrier, size - 1)
        send(k)

    feeds = slot_ref.shape[1]
    tile = min(TILE, feeds)
    for k in range(chunks - 1):
        arrive(k)
        depth = 2 * counts[k]
        set_left(left, hold_bufs[k], own_ref[...], scale)

        def columns(j, carry, k=k, depth=depth):
            where = pl.ds(pl.multiple_of(j * tile, tile), tile)
            ordered = pick(hold_bufs[k], slot_ref[:, where]).astype(jnp.bfloat16)
            for part in range(2):
                product = jnp.dot(left[part, :, :depth], ordered, preferred_element_type=jnp.float32)
                if k:
                    product = product + total[part, :, where]
                total[part, :, where] = product
            return carry

        lax.fori_loop(0, feeds // tile, columns, 0)
    total_copy = pltpu.make_async_copy(total, total_hbm, total_sem)
    total_copy.start()
    arrive(chunks - 1)
    for k in range(chunks):
        drain(k)
    total_copy.wait()


def exchange(words, gains, feed_slot, own, counts, inputs, groups, scale):
    size = CH * groups
    feeds = feed_slot.shape[0]
    wide = words.shape[2]
    bank = jnp.asarray(filter_bank())
    held = [jax.ShapeDtypeStruct((size, 2 * count, inputs), jnp.bfloat16) for count in counts]
    memory = pl.BlockSpec(memory_space=pltpu.VMEM)
    anywhere = pl.BlockSpec(memory_space=pl.ANY)
    chunks = len(counts)
    return pl.pallas_call(
        functools.partial(exchange_kernel, counts, groups, scale),
        out_shape=(held[-1], jax.ShapeDtypeStruct((2, ROWS, feeds), jnp.float32)),
        in_specs=[memory, anywhere, memory, memory, memory],
        out_specs=(anywhere, anywhere),
        scratch_shapes=[pltpu.VMEM((count + TAPS - 1, CH, wide), jnp.int32) for count in counts]
        + [pltpu.VMEM((CH, 2 * count, inputs), jnp.bfloat16) for count in counts]
        + [pltpu.VMEM(one.shape, one.dtype) for one in held[:-1]]
        + [
            pltpu.VMEM(((SPAN + TAPS) * 2 * CH, wide), jnp.bfloat16),
            pltpu.VMEM((2, wide // LANES, SPAN * CH, LANES), jnp.float32),
            pltpu.VMEM((2, ROWS, feeds), jnp.float32),
            pltpu.VMEM((2, ROWS, 2 * max(counts)), jnp.bfloat16),
            pltpu.SemaphoreType.DMA((chunks,)),
            pltpu.SemaphoreType.DMA((chunks,)),
            pltpu.SemaphoreType.DMA,
            pltpu.SemaphoreType.DMA((chunks, size)),
            pltpu.SemaphoreType.DMA((chunks, size)),
        ],
        compiler_params=pltpu.CompilerParams(
            collective_id=0, has_side_effects=True, vmem_limit_bytes=60 * 2**20
        ),
    )(bank, words, gains, feed_slot[None], own[None])


def finish_kernel(scale, moved_ref, slot_ref, own_ref, total_ref, out_ref, left):
    @pl.when(pl.program_id(0) == 0)
    def _():
        set_left(left, moved_ref, own_ref[...], scale)

    ordered = pick(moved_ref, slot_ref[...]).astype(jnp.bfloat16)
    for part in range(2):
        product = jnp.dot(left[part], ordered, preferred_element_type=jnp.float32)
        out_ref[:, part, :] = product + total_ref[part]


def split_kernel(counts, scale, bank_ref, words_hbm, gains_ref, slot_ref, *refs):
    chunks = len(counts)
    refs = list(refs)

    def take(count):
        taken = refs[:count]
        del refs[:count]
        return taken

    (raw_hbm,) = take(1)
    words_bufs = take(chunks)
    send_bufs = take(chunks)
    full_bufs = take(chunks)
    half_bufs = take(chunks)
    give_bufs = take(chunks)
    take_bufs = take(chunks)
    lefts = take(chunks)
    mine, given, voltage, rows, total, left = take(6)
    word_sem, own_sem, raw_sem, near_sems, cross_sems, row_sems, product_sems = refs
    me = lax.axis_index("feed")
    size = lax.axis_size("feed")
    half = size // 2
    core = me % 2
    base = me // half * half
    away = half - base
    spot = me - base
    mate = away + spot + 1 - 2 * core
    quarter = me // (size // 4)
    inner = (quarter + 1) // 2 % 2
    inputs = send_bufs[0].shape[2]
    bank = bank_ref[...]
    own = slot_ref[:, :ROWS]
    gain = gains_ref[...].astype(jnp.float32) * (1.0 / 2048.0)

    barrier = pltpu.get_barrier_semaphore()

    def greet(d, carry):
        pl.semaphore_signal(
            barrier, inc=1, device_id={"feed": (me + d) % size}, device_id_type=pl.DeviceIdType.MESH
        )
        return carry

    lax.fori_loop(1, size, greet, 0)

    def loop(first, last, step):
        def one(i, carry):
            step(i)
            return carry

        lax.fori_loop(first, last, one, 0)

    def word_copy(k):
        source = words_hbm.at[pl.ds(sum(counts[:k]), counts[k] + TAPS - 1)]
        return pltpu.make_async_copy(source, words_bufs[k], word_sem.at[k])

    def remote(source, target, sems, place, there):
        send_sem, recv_sem = sems
        return pltpu.make_async_remote_copy(
            src_ref=source,
            dst_ref=target,
            send_sem=send_sem.at[place],
            recv_sem=recv_sem.at[place],
            device_id={"feed": there},
            device_id_type=pl.DeviceIdType.MESH,
        )

    def channel(place):
        odd = place % 2
        return (base + place) * (1 - odd) + (away + place - 1) * odd

    def near(k, d):
        place = (spot + d) % half
        return remote(
            send_bufs[k].at[channel(place)], half_bufs[k].at[spot], near_sems, (k, d), base + place
        )

    def near_own(k):
        return pltpu.make_async_copy(send_bufs[k].at[channel(spot)], half_bufs[k].at[spot], own_sem.at[0, k])

    def far(k, i):
        there = away + (spot + i) % half
        return remote(send_bufs[k].at[there], full_bufs[k].at[me], cross_sems, (k, half + i), there)

    def close(k, i):
        there = base + (spot + i) % half
        return remote(send_bufs[k].at[there], full_bufs[k].at[me], cross_sems, (k, i), there)

    def cross_own(k):
        return pltpu.make_async_copy(send_bufs[k].at[me], full_bufs[k].at[me], own_sem.at[1, k])

    def row_copy(k):
        return remote(give_bufs[k], take_bufs[k], row_sems, k, mate)

    def product_copy(j):
        return remote(given.at[j], raw_hbm.at[base + j], product_sems, j, mate)

    def send_near(k):
        loop(1, half, lambda d: near(k, d).start())
        near_own(k).start()

    def arrive_near(k):
        near_own(k).wait()
        loop(1, half, lambda d: near(k, d).wait_recv())

    plane = half // 2

    def straight(k, q):
        return far(k, (q * plane + spot % plane // 2 * 2 + 1 - spot + half) % half)

    def across(k, q):
        return far(k, (q * plane + (spot + 2) % plane // 2 * 2 + 1 - spot + half) % half)

    def send_straight(k):
        loop(0, 2, lambda q: straight(k, q).start())

    def send_across(k):
        loop(0, 2, lambda q: across(k, q).start())

    def send_close(k):
        loop(core, half // 2, lambda q: close(k, 2 * q + 1 - core).start())

    senders = {"straight": send_straight, "across": send_across, "close": send_close}

    def issue(stage):
        for place, plan in ISSUE.items():
            steps = [step for step in plan if step[0] == stage]
            if steps:

                @pl.when((inner == place // 2) & (core == place % 2))
                def _(steps=steps):
                    for _, kind, k in steps:
                        senders[kind](k)

    def drain(k):
        loop(1, half, lambda d: near(k, d).wait_send())
        loop(0, half // 2, lambda q: far(k, 2 * q + 1 - core).wait_send())
        loop(core, half // 2, lambda q: close(k, 2 * q + 1 - core).wait_send())
        row_copy(k).wait_send()

    def arrive_cross(k):
        cross_own(k).start()
        cross_own(k).wait()
        loop(1, half, lambda i: close(k, i).wait_recv())
        loop(0, half, lambda i: far(k, i).wait_recv())

    word_copy(0).start()
    for k in range(chunks):
        word_copy(k).wait()
        if k + 1 < chunks:
            word_copy(k + 1).start()
        channelize(counts[k], bank, gain, words_bufs[k], send_bufs[k], voltage, rows)
        if k == 0:
            pl.semaphore_wait(barrier, size - 1)
        send_near(k)
        issue(k)

    for k in range(chunks):
        arrive_near(k)
        give_bufs[k][...] = pick(half_bufs[k], own, base * inputs).astype(jnp.bfloat16)
        row_copy(k).start()
        issue(ROW_STAGE + k)

    issue(ROWS_SENT)

    for k in range(chunks):
        row_copy(k).wait_recv()
        both = give_bufs[k][...].astype(jnp.float32) + take_bufs[k][...].astype(jnp.float32)
        put_left(lefts[k], both, scale)

    def raw_copy(buf, j, slot):
        return pltpu.make_async_copy(buf.at[slot], raw_hbm.at[j], raw_sem.at[j])

    def multiply(j):
        for part in range(2):
            product = None
            for k in range(chunks):
                term = jnp.dot(lefts[k][part], half_bufs[k][j], preferred_element_type=jnp.float32)
                product = term if product is None else product + term
            given[j, part * ROWS : (part + 1) * ROWS, :] = product.astype(jnp.bfloat16)

        @pl.when(core == 0)
        def _():
            raw_copy(given, base + j, j).start()

        @pl.when(core == 1)
        def _():
            product_copy(j).start()

    loop(0, half, multiply)
    issue(PRODUCTS_SENT)

    @pl.when(core == 0)
    def _():
        loop(0, half, lambda j: raw_copy(given, base + j, j).wait())
        loop(0, half, lambda j: product_copy(j).wait_recv())
        issue(PRODUCTS_HERE)

    @pl.when(core == 1)
    def _():
        for k in range(chunks):
            arrive_cross(k)
            depth = 2 * counts[k]
            set_left(left, full_bufs[k], own, scale)

            def block(j, k=k, depth=depth):
                for part in range(2):
                    rows = slice(part * ROWS, (part + 1) * ROWS)
                    product = jnp.dot(left[part, :, :depth], full_bufs[k][j], preferred_element_type=jnp.float32)
                    if k:
                        product = product + total[j, rows, :]
                    if k < chunks - 1:
                        total[j, rows, :] = product
                    else:
                        mine[j, rows, :] = product.astype(jnp.bfloat16)
                if k == chunks - 1:
                    raw_copy(mine, j, j).start()

            loop(0, size, block)
        loop(0, size, lambda j: raw_copy(mine, j, j).wait())
        loop(0, half, lambda j: product_copy(j).wait_send())

    for k in range(chunks):
        drain(k)


def split_exchange(words, gains, feed_slot, counts, inputs, scale):
    size = CH
    half = size // 2
    wide = words.shape[2]
    bank = jnp.asarray(filter_bank())
    memory = pl.BlockSpec(memory_space=pltpu.VMEM)
    anywhere = pl.BlockSpec(memory_space=pl.ANY)
    chunks = len(counts)
    half_type = jnp.bfloat16
    return pl.pallas_call(
        functools.partial(split_kernel, counts, scale),
        out_shape=jax.ShapeDtypeStruct((size, 2 * ROWS, inputs), half_type),
        in_specs=[memory, anywhere, memory, memory],
        out_specs=anywhere,
        scratch_shapes=[pltpu.VMEM((count + TAPS - 1, CH, wide), jnp.int32) for count in counts]
        + [pltpu.VMEM((CH, 2 * count, inputs), half_type) for count in counts]
        + [pltpu.VMEM((size, 2 * count, inputs), half_type) for count in counts]
        + [pltpu.VMEM((half, 2 * count, inputs), half_type) for count in counts]
        + [pltpu.VMEM((2 * count, ROWS), half_type) for count in counts] * 2
        + [pltpu.VMEM((2, ROWS, 2 * count), half_type) for count in counts]
        + [
            pltpu.VMEM((size, 2 * ROWS, inputs), half_type),
            pltpu.VMEM((half, 2 * ROWS, inputs), half_type),
            pltpu.VMEM(((SPAN + TAPS) * 2 * CH, wide), half_type),
            pltpu.VMEM((2, wide // LANES, SPAN * CH, LANES), jnp.float32),
            pltpu.VMEM((size, 2 * ROWS, inputs), jnp.float32),
            pltpu.VMEM((2, ROWS, 2 * max(counts)), half_type),
            pltpu.SemaphoreType.DMA((chunks,)),
            pltpu.SemaphoreType.DMA((2, chunks)),
            pltpu.SemaphoreType.DMA((size,)),
            (pltpu.SemaphoreType.DMA((chunks, half)),) * 2,
            (pltpu.SemaphoreType.DMA((chunks, size)),) * 2,
            (pltpu.SemaphoreType.DMA((chunks,)),) * 2,
            (pltpu.SemaphoreType.DMA((half,)),) * 2,
        ],
        compiler_params=pltpu.CompilerParams(
            collective_id=0, has_side_effects=True, vmem_limit_bytes=60 * 2**20
        ),
    )(bank, words, gains, feed_slot[None])


def turn(block):
    size = block.shape[1]
    down = lax.broadcasted_iota(jnp.int32, (size, size), 0)
    along = lax.broadcasted_iota(jnp.int32, (size, size), 1)
    same = jnp.where(down == along, 1.0, 0.0).astype(jnp.bfloat16)
    return lax.dot_general(same, block, (((1,), (1,)), ((), ())), preferred_element_type=jnp.float32)


def split_finish_kernel(raw_hbm, slot_ref, out_ref, raw, table, even, odd, sems):
    sources, depth, width = raw.shape
    pieces = depth // LANES
    per = ROWS // LANES
    tile = out_ref.shape[2]
    first = pl.program_id(0) * tile
    step = even.shape[0] // pieces

    def raw_copy(source):
        return pltpu.make_async_copy(raw_hbm.at[source], raw.at[source], sems.at[source])

    @pl.when(pl.program_id(0) == 0)
    def _():
        def begin(source, carry):
            raw_copy(source).start()
            return carry

        def fill(source, carry):
            raw_copy(source).wait()
            turned = turn(raw[source])
            for piece in range(pieces):
                where = pl.ds(source * width * pieces + piece, width, stride=pieces)
                table[where, :] = turned[:, piece * LANES : (piece + 1) * LANES]
            return carry

        lax.fori_loop(0, sources, begin, 0)
        lax.fori_loop(0, sources, fill, 0)

    def gather(picked, begin):
        for place in range(step):
            slot = slot_ref[0, first + begin + place]
            row = table[pl.ds(pl.multiple_of(slot * pieces, pieces), pieces), :]
            picked[place * pieces : (place + 1) * pieces, :] = row

    def put(picked, begin):
        for part in range(2):
            rows = [picked[pl.ds(part * per + piece, step, stride=pieces), :] for piece in range(per)]
            turned = turn(jnp.concatenate(rows, axis=1).astype(jnp.bfloat16))
            out_ref[:, part, begin : begin + step] = turned

    gather(even, 0)
    for i in range(tile // step):
        here, there = (even, odd) if i % 2 == 0 else (odd, even)
        if i + 1 < tile // step:
            gather(there, (i + 1) * step)
        put(here, i * step)


def split_finish(raw, feed_slot):
    sources, depth, width = raw.shape
    feeds = feed_slot.shape[0]
    tile = min(FINISH_TILE, feeds)
    step = min(STEP, tile)
    pieces = depth // LANES
    return pl.pallas_call(
        split_finish_kernel,
        out_shape=jax.ShapeDtypeStruct((ROWS, 2, feeds), jnp.float32),
        grid=(feeds // tile,),
        in_specs=[pl.BlockSpec(memory_space=pl.ANY), pl.BlockSpec(memory_space=pltpu.SMEM)],
        out_specs=pl.BlockSpec((ROWS, 2, tile), lambda j: (0, 0, j)),
        scratch_shapes=[
            pltpu.VMEM(raw.shape, raw.dtype),
            pltpu.VMEM((sources * width * pieces, LANES), jnp.float32),
            pltpu.VMEM((step * pieces, LANES), jnp.float32),
            pltpu.VMEM((step * pieces, LANES), jnp.float32),
            pltpu.SemaphoreType.DMA((sources,)),
        ],
    )(raw, feed_slot[None])


def finish(moved, feed_slot, own, total, scale):
    feeds = feed_slot.shape[0]
    tile = min(TILE, feeds)
    return pl.pallas_call(
        functools.partial(finish_kernel, scale),
        out_shape=jax.ShapeDtypeStruct((ROWS, 2, feeds), jnp.float32),
        grid=(feeds // tile,),
        in_specs=[
            pl.BlockSpec(moved.shape, lambda j: (0, 0, 0)),
            pl.BlockSpec((1, tile), lambda j: (0, j)),
            pl.BlockSpec((1, ROWS), lambda j: (0, 0)),
            pl.BlockSpec((2, ROWS, tile), lambda j: (0, 0, j)),
        ],
        out_specs=pl.BlockSpec((ROWS, 2, tile), lambda j: (0, 0, j)),
        scratch_shapes=[pltpu.VMEM((2, ROWS, moved.shape[1]), jnp.bfloat16)],
    )(moved, feed_slot[None], own[None], total)


def body(samples, gains, feed_slot):
    groups = lax.axis_size("feed") // CH
    first = lax.axis_index("feed") % groups * ROWS
    inputs = samples.shape[0]
    spectra = samples.shape[2] - TAPS + 1
    split = groups == 1 and inputs % LANES == 0
    shares = SPLIT_SHARES if split else SHARES
    counts = tuple(spectra * share // sum(shares) for share in shares)
    words = jnp.transpose(samples, (2, 1, 0))
    spare = -inputs % LANES
    if spare:
        words = jnp.pad(words, ((0, 0), (0, 0), (0, spare)))
        gains = jnp.pad(gains, ((0, 0), (0, 0), (0, spare)))
    scale = 1.0 / spectra
    if split:
        raw = split_exchange(words, gains, feed_slot, counts, inputs, scale)
        return split_finish(raw, feed_slot)
    own = lax.dynamic_slice_in_dim(feed_slot, first, ROWS, 0)
    moved, total = exchange(words, gains, feed_slot, own, counts, inputs, groups, scale)
    return finish(moved, feed_slot, own, total, scale)


def solution(mesh):
    return jax.shard_map(
        body,
        mesh=mesh,
        in_specs=(P(("band", "feed"), None, None), P(None, "band", "feed"), P()),
        out_specs=P(("band", "feed"), None, None),
        check_vma=False,
    )
```
